32 devices in a mesh: group: 2 (over x), ccd: 16 (over z, y, core).
Axes of the slice: x: 2, y: 2, z: 4, core: 2. Of those that a mesh axis runs over, the one named last changes fastest.
Arguments:
- images: float32 [4, 4096, 512], P(None, ('group', 'ccd')), parts along dimension 1, may hold values from -6 to 6
- basis_taps: float32 [2, 9, 11], replicated, may hold values from -1.75 to 1.75
- psf_coef: float32 [4, 10, 9, 3], P(None, 'group'), parts along dimension 1, may hold values from -3 to 3
- affine: float32 [4, 10, 2, 2], P(None, 'group'), parts along dimension 1, may hold values from -0.5 to 0.5
- visit_weight: bfloat16 [4, 10], P(None, 'group'), parts along dimension 1, may hold values from 0.25 to 4
- block_patch: int32 [32, 16, 1], P(('group', 'ccd')), parts along dimension 0, may hold values from 0 to 15; in each aligned block of 16 rows (0 to 15, 16 to 31, ..., all dimensions but the last counted through in order) at most 2 rows name the same one
- block_slot: int32 [32, 16], P(('group', 'ccd')), parts along dimension 0, may hold values from 0 to 15
- patch_owner: int32 [32], P('group'), parts along dimension 0, may hold values from 0 to 15, each once
Outputs:
- coadd: float32 [32, 512, 512], P(('group', 'ccd')), parts along dimension 0
The draws below stay inside these ranges and needn't reach their ends.
There are 2 independent parts, one for each index of `group`. The reference program is written for one: setup_inputs(seed, part) draws one part's arguments, and reference() takes and returns one part's arrays. A program takes and returns all parts, laid end to end along the dimension named above; an argument that names none is the same for every part. Nothing has to cross between parts.
Inputs may be any that keep to these rules, and one draw needn't show every extreme that they name: `block_patch`: among the 16 blocks of one band no patch is named more than 2 times, and in every draw some band names some patch exactly 2 times. `patch_owner`: each device index along ccd owns exactly one patch.
All inputs are finite; a program needn't handle non-finite values.
Results may differ from the reference program's by a relative error of at most 0.0029.
Values may be sent and summed in bfloat16 or wider, within the bound.
A program may use at most 64 MiB of HBM per device.

```python
import math
import jax
import jax.numpy as jnp
import numpy as np
from jax import lax

V = 4
BLOCK = 128
BLKC = 4
SPLIT = 4
TAPS = 11
NBASIS = 9
PSIDE = 4
BANDS = 16
NCCD = 5
NPATCH = 16
BLK_DEV = 16
CAP = 2


def touch_ends(result, own_key, low, high):
    place = [jax.random.randint(jax.random.fold_in(own_key, axis), (), 0, length) for axis, length in enumerate(result.shape)]
    longest = result.shape.index(max(result.shape))
    beside = place[:longest] + [(place[longest] + 1) % result.shape[longest]] + place[longest + 1:]
    return result.at[tuple(place)].set(low).at[tuple(beside)].set(high)


def level_of(own_key, extent, pieces, low, largest):
    def one(axis_at, parts):
        draws = jax.random.uniform(jax.random.fold_in(jax.random.fold_in(own_key, 6), axis_at), (parts,), jnp.float32, low / len(pieces), largest / len(pieces))
        return jnp.repeat(jnp.exp(draws), extent[axis_at] // parts).reshape((-1,) + (1,) * (len(extent) - axis_at - 1))

    level = one(*pieces[0])
    for cut in pieces[1:]:
        level = level * one(*cut)
    return level


def shared_out(rng, own, number, rows, amount, top, limit, lean):
    ranking = jax.random.permutation(rng, amount)
    crowded, usual = shares(amount, rows * top, limit, lean, True), shares(amount, rows * top, limit, lean, False)
    places = jnp.arange(amount)

    def named(lengths, offset_by):
        used = int((lengths > 0).sum())
        fixed = max(1, used // 4)
        passed = fixed + (places - fixed + offset_by * (used - fixed)) % max(1, amount - fixed)
        return jnp.zeros((amount,), jnp.int32).at[ranking[jnp.where(places < fixed, places, passed)]].set(jnp.asarray(lengths, jnp.int32))

    lengths = jnp.where(number % 4 == 0, named(crowded, number // 4), named(usual, number - number // 4 - 1))
    mixed = jax.random.permutation(jax.random.fold_in(own, 3), amount)
    source_of, taker = mixed[0:amount // 2 * 2:2], mixed[1:amount // 2 * 2:2]
    margin = jnp.minimum(lengths[source_of] - 1, limit - lengths[taker]) // 2
    margin = jnp.where((source_of == ranking[0]) | (taker == ranking[0]) | (lengths[taker] == 0), 0, jnp.maximum(margin, 0))
    passed = jax.random.randint(jax.random.fold_in(own, 4), (amount // 2,), 0, 1 << 20) % (margin + 1)
    lengths = lengths.at[source_of].add(-passed).at[taker].add(passed)
    labels = jnp.searchsorted(jnp.cumsum(lengths), jnp.arange(rows * top), side="right").astype(jnp.int32)
    listing = labels.reshape(top, rows).T
    listing = listing[jax.random.permutation(jax.random.fold_in(own, 1), rows)]
    offset_by = jax.random.randint(jax.random.fold_in(own, 2), (rows, 1), 0, top)
    return jnp.take_along_axis(listing, (jnp.arange(top)[None, :] + offset_by) % top, axis=1)


def shares(count, total, most, slope, full):
    weights = [(1 << 20) // math.isqrt(grade ** slope) + 1 for grade in range(1, count + 1)]
    largest = most if full else min(most, max(-(-total // count), total * weights[0] // sum(weights)))
    least = 1 if total - largest >= count - 1 else 0
    given, surplus = [largest] + [least] * (count - 1), total - largest - least * (count - 1)
    while surplus > 0:
        candidates = [i for i in range(1, count) if given[i] < largest] or [i for i in range(1, count) if given[i] < most]
        pool, left = sum([weights[i] for i in candidates]), surplus
        for i in candidates:
            more = min(most - given[i], max(1, left * weights[i] // pool), surplus)
            given[i] = given[i] + more
            surplus = surplus - more
    return np.array(given)


def bell_draw(rng, shape, spread, most, cuts=(), kind=jnp.bfloat16):
    values = spread * jax.random.normal(rng, shape, jnp.float32)
    if cuts:
        values = values * level_of(rng, shape, cuts, -0.22, 0.18)
    return jnp.clip(values, -most, most).astype(kind)


def setup_inputs(seed: int = 0, part: int = 0) -> dict:
    splits = jax.random.split(jax.random.key(seed), 9)
    part_splits = jax.random.split(jax.random.fold_in(splits[8], part), 9)
    images = bell_draw(part_splits[0], (V, BANDS * BLOCK, BLKC * BLOCK), 1.0, 6.0, ((1, 16),), jnp.float32)
    basis_taps = bell_draw(splits[1], (2, NBASIS, TAPS), TAPS ** -0.5, 1.75, (), jnp.float32)
    psf_coef = bell_draw(part_splits[2], (V, NCCD, NBASIS, 3), 0.35, 3.0, (), jnp.float32)
    affine = jnp.clip(jax.random.uniform(part_splits[3], (V, NCCD, 2, 2), jnp.float32, -0.5, 0.5), -0.5, 0.5)
    visit_weight = jnp.clip(jnp.exp(jax.random.uniform(part_splits[4], (V, NCCD), jnp.float32, math.log(0.25), math.log(4.0))), 0.25, 4.0).astype(jnp.bfloat16)
    block_patch_keys = jax.random.split(jax.random.fold_in(part_splits[5], 1), BANDS * BLK_DEV // BLK_DEV)
    block_patch_turns = jax.random.permutation(jax.random.fold_in(part_splits[5], 3), BANDS * BLK_DEV // BLK_DEV)
    block_patch = jax.vmap(lambda own, number: shared_out(jax.random.fold_in(part_splits[5], 2), own, number, BLK_DEV, NPATCH, 1, CAP, 2))(block_patch_keys, block_patch_turns).reshape((BANDS, BLK_DEV, 1))
    block_slot = touch_ends(jax.random.randint(part_splits[6], (BANDS, BLK_DEV), 0, PSIDE * PSIDE), jax.random.fold_in(part_splits[6], 1), 0, (PSIDE * PSIDE) - 1).astype(jnp.int32)
    patch_owner = jax.random.permutation(part_splits[7], NPATCH).astype(jnp.int32)
    return {"images": images, "basis_taps": basis_taps, "psf_coef": psf_coef, "affine": affine, "visit_weight": visit_weight, "block_patch": block_patch, "block_slot": block_slot, "patch_owner": patch_owner}


def lanczos(offset):
    inside = jnp.abs(offset) < 3.0
    return jnp.where(inside, jnp.sinc(offset) * jnp.sinc(offset / 3.0), 0.0)


def match_warp(inputs, basis_taps):
    ccd_image, psf_terms, affine_map, ccd_number = inputs
    height = SPLIT * BLOCK
    ccd_width = BLKC * BLOCK
    half_taps = TAPS // 2
    offset_rows = (SPLIT // 2) * BLOCK
    row_pos = (2.0 * jnp.arange(height, dtype=jnp.float32) + 1.0) / height - 1.0
    col_pos = (2.0 * jnp.arange(ccd_width, dtype=jnp.float32) + 1.0) / ccd_width - 1.0
    padded = jnp.pad(ccd_image, ((0, 0), (half_taps, half_taps)))
    matched = jnp.zeros((height, ccd_width), jnp.float32)
    for basis_index in range(NBASIS):
        column_pass = jnp.zeros((height, ccd_width), jnp.float32)
        for tap_index in range(TAPS):
            column_pass = column_pass + basis_taps[1, basis_index, tap_index] * padded[:, tap_index:tap_index + ccd_width]
        row_padded = jnp.pad(column_pass, ((half_taps, half_taps), (0, 0)))
        row_pass = jnp.zeros((height, ccd_width), jnp.float32)
        for tap_index in range(TAPS):
            row_pass = row_pass + basis_taps[0, basis_index, tap_index] * row_padded[tap_index:tap_index + height]
        spatial = psf_terms[basis_index, 0] + psf_terms[basis_index, 1] * row_pos[:, None] + psf_terms[basis_index, 2] * col_pos[None, :]
        matched = matched + spatial * row_pass
    region_row = ccd_number * height + jnp.arange(height, dtype=jnp.int32) - offset_rows
    keep = ((region_row >= 0) & (region_row < BANDS * BLOCK)).astype(jnp.float32)
    matched = matched * keep[:, None]
    rows_global = jnp.arange(height, dtype=jnp.float32)
    row_shift = affine_map[0, 0] + affine_map[0, 1] * (rows_global - (height - 1) / 2.0) / height
    framed = jnp.pad(matched, ((3, 3), (0, 0)))
    row_warped = jnp.zeros((height, ccd_width), jnp.float32)
    for step_index in range(-3, 4):
        row_warped = row_warped + lanczos(row_shift - step_index)[:, None] * framed[3 + step_index:3 + step_index + height]
    cols_global = jnp.arange(ccd_width, dtype=jnp.float32)
    col_shift = affine_map[1, 0] + affine_map[1, 1] * (cols_global - (ccd_width - 1) / 2.0) / ccd_width
    framed_cols = jnp.pad(row_warped, ((0, 0), (3, 3)))
    warped = jnp.zeros((height, ccd_width), jnp.float32)
    for step_index in range(-3, 4):
        warped = warped + lanczos(col_shift - step_index)[None, :] * framed_cols[:, 3 + step_index:3 + step_index + ccd_width]
    return warped.astype(jnp.bfloat16)


def reference(images, basis_taps, psf_coef, affine, visit_weight, block_patch, block_slot, patch_owner):
    height = SPLIT * BLOCK
    ccd_width = BLKC * BLOCK
    offset_rows = (SPLIT // 2) * BLOCK
    tail_rows = NCCD * height - BANDS * BLOCK - offset_rows
    padded_images = jnp.pad(images, ((0, 0), (offset_rows, tail_rows), (0, 0)))
    stacked = padded_images.reshape(V * NCCD, height, ccd_width)
    psf_terms = psf_coef.reshape(V * NCCD, NBASIS, 3)
    affine_maps = affine.reshape(V * NCCD, 2, 2)
    ccd_numbers = jnp.tile(jnp.arange(NCCD, dtype=jnp.int32), V)

    def one_ccd(inputs):
        return match_warp(inputs, basis_taps)

    warped = lax.map(one_ccd, (stacked, psf_terms, affine_maps, ccd_numbers))
    warped = warped.reshape(V, NCCD * height, ccd_width)[:, offset_rows:offset_rows + BANDS * BLOCK]
    blocks = warped.reshape(V, BANDS, BLOCK, BLKC, BLOCK).transpose(1, 0, 3, 2, 4)
    blocks = blocks.reshape(BANDS * V * BLKC, BLOCK * BLOCK)
    band_ccd = (jnp.arange(BANDS, dtype=jnp.int32) + SPLIT // 2) // SPLIT
    weights = visit_weight.astype(jnp.float32).T[band_ccd]
    weights = jnp.repeat(weights, BLKC, axis=1).reshape(-1)
    cells = PSIDE * PSIDE
    segment_ids = (block_patch[:, :, 0] * cells + block_slot).reshape(-1).astype(jnp.int32)
    contrib = weights[:, None] * blocks.astype(jnp.float32)
    numerator = jax.ops.segment_sum(contrib, segment_ids, num_segments=NPATCH * cells)
    denominator = jax.ops.segment_sum(weights, segment_ids, num_segments=NPATCH * cells)
    patches = numerator / jnp.maximum(denominator, 1.0)[:, None]
    patches = patches.reshape(NPATCH, PSIDE, PSIDE, BLOCK, BLOCK).transpose(0, 1, 3, 2, 4)
    patches = patches.reshape(NPATCH, PSIDE * BLOCK, PSIDE * BLOCK)
    coadd = jnp.zeros_like(patches).at[patch_owner].set(patches)
    return coadd
```

```python
import functools

import jax
import jax.numpy as jnp
from jax import lax
from jax.experimental import pallas as pl
from jax.experimental.pallas import tpu as pltpu
from jax.sharding import PartitionSpec as P

V = 4
BLOCK = 128
BLKC = 4
SPLIT = 4
TAPS = 11
NBASIS = 9
PSIDE = 4
HALF = TAPS // 2
REACH = 3
RIM = HALF + REACH
ROWS_IN = BLOCK + 2 * RIM
ROWS_MID = BLOCK + 8
WIDTH = BLKC * BLOCK
HEIGHT = SPLIT * BLOCK
LEFT = BLOCK // 2
STEPS = 2 * REACH + 1


def lanczos(offset):
    inside = jnp.abs(offset) < 3.0
    return jnp.where(inside, jnp.sinc(offset) * jnp.sinc(offset / 3.0), 0.0)


def split(values):
    high = values.astype(jnp.bfloat16)
    return high, (values - high.astype(jnp.float32)).astype(jnp.bfloat16)


def dot(left, right):
    return jnp.dot(left, right, preferred_element_type=jnp.float32)


def band_kernel(
    target_ref,
    top_ref,
    above_ref,
    image_ref,
    below_ref,
    col_taps_ref,
    row_taps_ref,
    row_index_ref,
    coef_ref,
    row_weight_ref,
    col_weight_ref,
    send_ref,
    col_high,
    col_low,
    row_kernel,
    wide,
    terms_high,
    terms_low,
    mid,
):
    visit = pl.program_id(0)
    top_row = top_ref[0]
    region_low = top_ref[1]
    region_high = top_ref[2]

    @pl.when(visit == 0)
    def _():
        send_ref[...] = jnp.zeros_like(send_ref)
        depth = lax.broadcasted_iota(jnp.int32, (2 * BLOCK, BLOCK), 0)
        lane = lax.broadcasted_iota(jnp.int32, (2 * BLOCK, BLOCK), 1)
        distance = depth - (LEFT - HALF) - lane
        for basis in range(NBASIS):
            cols = pl.ds(basis * BLOCK, BLOCK)
            total = jnp.zeros((2 * BLOCK, BLOCK), jnp.float32)
            for tap in range(TAPS):
                total = jnp.where(distance == tap, col_taps_ref[tap : tap + 1, cols], total)
            high, low = split(total)
            col_high[:, cols] = high
            col_low[:, cols] = low
        gap = row_index_ref[...] - lax.broadcasted_iota(
            jnp.int32, (ROWS_MID, NBASIS * ROWS_IN), 0
        )
        total = jnp.zeros(gap.shape, jnp.float32)
        for tap in range(TAPS):
            total = jnp.where(gap == tap, row_taps_ref[tap : tap + 1, :], total)
        row_kernel[...] = total
        wide[...] = jnp.zeros_like(wide)

    def inside(first, count):
        rows = first + lax.broadcasted_iota(jnp.int32, (count, 1), 0)
        return (rows >= region_low) & (rows < region_high)

    raw = jnp.concatenate([above_ref[0], image_ref[0], below_ref[0]], axis=0)
    raw = jnp.where(inside(top_row - RIM, ROWS_IN), raw, 0.0)
    wide[:, LEFT : LEFT + WIDTH] = raw
    for block in range(BLKC):
        high, low = split(wide[:, block * BLOCK : (block + 2) * BLOCK])
        term = dot(high, col_high[...]) + dot(low, col_high[...]) + dot(high, col_low[...])
        high, low = split(term)
        for basis in range(NBASIS):
            rows = pl.ds(basis * ROWS_IN, ROWS_IN)
            cols = pl.ds(block * BLOCK, BLOCK)
            terms_high[rows, cols] = high[:, basis * BLOCK : (basis + 1) * BLOCK]
            terms_low[rows, cols] = low[:, basis * BLOCK : (basis + 1) * BLOCK]

    position = (top_row - REACH + lax.broadcasted_iota(jnp.int32, (ROWS_MID, 1), 0)).astype(
        jnp.float32
    )
    row_pos = (2.0 * position + 1.0) / HEIGHT - 1.0
    column = lax.broadcasted_iota(jnp.int32, (1, WIDTH), 1).astype(jnp.float32)
    col_pos = (2.0 * column + 1.0) / WIDTH - 1.0
    kernel = row_kernel[...]
    level = kernel * (coef_ref[0, 0:1, :] + coef_ref[0, 1:2, :] * row_pos)
    slope = kernel * coef_ref[0, 2:3, :]
    level_high, level_low = split(level)
    slope_high, slope_low = split(slope)
    upper = dot(
        jnp.concatenate([level_high, slope_high, level_low, slope_low], axis=0), terms_high[...]
    )
    lower = dot(jnp.concatenate([level_high, slope_high], axis=0), terms_low[...])
    both = upper[: 2 * ROWS_MID] + upper[2 * ROWS_MID :] + lower
    matched = both[:ROWS_MID] + both[ROWS_MID:] * col_pos
    mid[...] = jnp.where(inside(top_row - REACH, ROWS_MID), matched, 0.0)

    warped = jnp.zeros((BLOCK, WIDTH), jnp.float32)
    for step in range(STEPS):
        warped = warped + row_weight_ref[0, :, step : step + 1] * mid[step : step + BLOCK, :]
    total = jnp.zeros((BLOCK, WIDTH), jnp.float32)
    for step in range(STEPS):
        offset = step - REACH
        moved = warped if offset == 0 else pltpu.roll(warped, (-offset) % WIDTH, 1)
        total = total + col_weight_ref[0, step : step + 1, :] * moved
    rounded = total.astype(jnp.bfloat16)
    for block in range(BLKC):
        send_ref[target_ref[visit * BLKC + block]] = rounded[
            :, block * BLOCK : (block + 1) * BLOCK
        ]


def gather_kernel(count, cell_ref, weight_ref, got_ref, out_ref, total, weights):
    total[...] = jnp.zeros_like(total)
    for cell in range(PSIDE * PSIDE):
        weights[cell] = 0.0

    def add(index, carry):
        cell = cell_ref[index]

        @pl.when(cell >= 0)
        def _():
            weight = weight_ref[index]
            weights[cell] = weights[cell] + weight
            total[cell] = total[cell] + weight * got_ref[index].astype(jnp.float32)

        return carry

    lax.fori_loop(0, count, add, 0)
    for cell in range(PSIDE * PSIDE):
        row, col = cell // PSIDE * BLOCK, cell % PSIDE * BLOCK
        scale = jnp.full((1, BLOCK), jnp.maximum(weights[cell], 1.0), jnp.float32)
        out_ref[0, row : row + BLOCK, col : col + BLOCK] = total[cell] / scale


def shards(
    images, basis_taps, psf_coef, affine, visit_weight, block_patch, block_slot, patch_owner
):
    band_index = lax.axis_index("ccd")
    devices = lax.axis_size("ccd")
    ends = devices - 1
    above = lax.ppermute(
        images[:, BLOCK - RIM :], "ccd", [(i, i + 1) for i in range(ends)]
    )
    below = lax.ppermute(images[:, :RIM], "ccd", [(i + 1, i) for i in range(ends)])
    shifted_band = band_index + SPLIT // 2
    ccd_index = shifted_band // SPLIT
    top_row = shifted_band % SPLIT * BLOCK
    region_shift = band_index * BLOCK - top_row
    limits = jnp.stack(
        [
            top_row,
            jnp.maximum(0, -region_shift),
            jnp.minimum(HEIGHT, devices * BLOCK - region_shift),
        ]
    ).astype(jnp.int32)

    block_count = V * BLKC
    capacity = max(2, (2 * block_count + devices - 1) // devices)
    slots = devices * capacity
    patch_ids = block_patch[0, :, 0]
    owner_match = patch_ids[:, None] == jnp.arange(patch_owner.shape[0])[None, :]
    destination = jnp.sum(jnp.where(owner_match, patch_owner[None, :], 0), axis=1)
    order = jnp.arange(block_count)
    same_owner = destination[:, None] == destination[None, :]
    rank = jnp.sum((same_owner & (order[None, :] < order[:, None])).astype(jnp.int32), axis=1)
    target = (destination * capacity + rank).astype(jnp.int32)
    hit = target[None, :] == jnp.arange(slots)[:, None]
    code = block_slot[0] * V + order // BLKC
    codes = jnp.sum(jnp.where(hit, code[None, :] + 1, 0), axis=1) - 1
    got_codes = lax.all_to_all(
        codes.reshape(devices, capacity), "ccd", split_axis=0, concat_axis=0, tiled=True
    )

    terms_here = lax.dynamic_index_in_dim(psf_coef, ccd_index, 1, keepdims=False)
    affine_here = lax.dynamic_index_in_dim(affine, ccd_index, 1, keepdims=False)
    coef = jnp.repeat(terms_here.transpose(0, 2, 1), ROWS_IN, axis=2)
    col_taps = jnp.repeat(basis_taps[1].T, BLOCK, axis=1)
    row_taps = jnp.repeat(basis_taps[0].T, ROWS_IN, axis=1)
    row_index = (jnp.arange(NBASIS * ROWS_IN, dtype=jnp.int32) % ROWS_IN)[None]
    steps = jnp.arange(STEPS) - REACH
    rows = (top_row + jnp.arange(BLOCK)).astype(jnp.float32)
    row_shift = affine_here[:, 0, 0:1] + affine_here[:, 0, 1:2] * (
        (rows - (HEIGHT - 1) / 2.0) / HEIGHT
    )
    row_weight = lanczos(row_shift[:, :, None] - steps.astype(jnp.float32))
    cols = jnp.arange(WIDTH)
    col_shift = affine_here[:, 1, 0:1] + affine_here[:, 1, 1:2] * (
        (cols.astype(jnp.float32) - (WIDTH - 1) / 2.0) / WIDTH
    )
    reached = cols[None, :] + steps[:, None]
    col_weight = jnp.where(
        (reached >= 0) & (reached < WIDTH),
        lanczos(col_shift[:, None, :] - steps.astype(jnp.float32)[:, None]),
        0.0,
    )

    def per_visit(shape):
        return pl.BlockSpec((1,) + shape[1:], lambda v, *_: (v, 0, 0))

    def whole(shape):
        return pl.BlockSpec(shape, lambda v, *_: (0,) * len(shape))

    out_shape = (slots, BLOCK, BLOCK)
    send = pl.pallas_call(
        band_kernel,
        out_shape=jax.ShapeDtypeStruct(out_shape, jnp.bfloat16),
        grid_spec=pltpu.PrefetchScalarGridSpec(
            num_scalar_prefetch=2,
            grid=(V,),
            in_specs=[
                per_visit(above.shape),
                per_visit(images.shape),
                per_visit(below.shape),
                whole(col_taps.shape),
                whole(row_taps.shape),
                whole(row_index.shape),
                per_visit(coef.shape),
                per_visit(row_weight.shape),
                per_visit(col_weight.shape),
            ],
            out_specs=whole(out_shape),
            scratch_shapes=[
                pltpu.VMEM((2 * BLOCK, NBASIS * BLOCK), jnp.bfloat16),
                pltpu.VMEM((2 * BLOCK, NBASIS * BLOCK), jnp.bfloat16),
                pltpu.VMEM((ROWS_MID, NBASIS * ROWS_IN), jnp.float32),
                pltpu.VMEM((ROWS_IN, WIDTH + BLOCK), jnp.float32),
                pltpu.VMEM((NBASIS * ROWS_IN, WIDTH), jnp.bfloat16),
                pltpu.VMEM((NBASIS * ROWS_IN, WIDTH), jnp.bfloat16),
                pltpu.VMEM((ROWS_MID, WIDTH), jnp.float32),
            ],
        ),
        compiler_params=pltpu.CompilerParams(dimension_semantics=("arbitrary",)),
    )(
        target,
        limits,
        above,
        images,
        below,
        col_taps,
        row_taps,
        row_index,
        coef,
        row_weight,
        col_weight,
    )
    got = lax.all_to_all(
        send.reshape(devices, capacity, BLOCK, BLOCK),
        "ccd",
        split_axis=0,
        concat_axis=0,
        tiled=True,
    ).reshape(out_shape)
    source_ccd = (jnp.arange(devices) + SPLIT // 2) // SPLIT
    by_source = visit_weight.astype(jnp.float32).T[source_ccd]
    used = got_codes >= 0
    cell = jnp.where(used, got_codes // V, -1).reshape(slots)
    which = jnp.arange(V)[None, None, :] == (got_codes % V)[:, :, None]
    weight = jnp.sum(jnp.where(which, by_source[:, None, :], 0.0), axis=2).reshape(slots)
    size = PSIDE * BLOCK
    return pl.pallas_call(
        functools.partial(gather_kernel, slots),
        out_shape=jax.ShapeDtypeStruct((1, size, size), jnp.float32),
        in_specs=[
            pl.BlockSpec(memory_space=pltpu.SMEM),
            pl.BlockSpec(memory_space=pltpu.SMEM),
            pl.BlockSpec(memory_space=pltpu.VMEM),
        ],
        out_specs=pl.BlockSpec(memory_space=pltpu.VMEM),
        scratch_shapes=[
            pltpu.VMEM((PSIDE * PSIDE, BLOCK, BLOCK), jnp.float32),
            pltpu.SMEM((PSIDE * PSIDE,), jnp.float32),
        ],
    )(cell, weight, got)


def solution(mesh):
    placed = (
        P(None, ("group", "ccd"), None),
        P(),
        P(None, "group", None, None),
        P(None, "group", None, None),
        P(None, "group"),
        P(("group", "ccd"), None, None),
        P(("group", "ccd"), None),
        P("group"),
    )
    return jax.shard_map(
        shards,
        mesh=mesh,
        in_specs=placed,
        out_specs=P(("group", "ccd"), None, None),
        check_vma=False,
    )
```

```python
import functools

import jax
import jax.numpy as jnp
from jax import lax
from jax.experimental import pallas as pl
from jax.experimental.pallas import tpu as pltpu
from jax.sharding import PartitionSpec as P

V = 4
BLOCK = 128
BLKC = 4
SPLIT = 4
TAPS = 11
NBASIS = 9
PSIDE = 4
HALF = TAPS // 2
REACH = 3
RIM = HALF + REACH
ROWS_IN = BLOCK + 2 * RIM
ROWS_MID = BLOCK + 8
WIDTH = BLKC * BLOCK
HEIGHT = SPLIT * BLOCK
LEFT = BLOCK // 2
STEPS = 2 * REACH + 1


def sinc(values):
    angle = jnp.pi * values
    zero = values == 0.0
    return jnp.where(zero, 1.0, jnp.sin(angle) / jnp.where(zero, 1.0, angle))


def lanczos(offset):
    inside = jnp.abs(offset) < 3.0
    return jnp.where(inside, sinc(offset) * sinc(offset / 3.0), 0.0)


def outward(count):
    return sorted(range(1, count), key=lambda step: abs(step - count // 2))


def meet(me, count):
    barrier = pltpu.get_barrier_semaphore()
    for step in range(1, count):
        pl.semaphore_signal(
            barrier,
            inc=1,
            device_id={"ccd": lax.rem(me + step, count)},
            device_id_type=pl.DeviceIdType.MESH,
        )
    pl.semaphore_wait(barrier, count - 1)


def rim_kernel(count, image_ref, meta_ref, above_ref, below_ref, metas_ref, sent, received, rims, own):
    me = lax.axis_index("ccd")
    meet(me, count)

    def remote(source, target, send, receive, step):
        return pltpu.make_async_remote_copy(
            src_ref=source,
            dst_ref=target,
            send_sem=send,
            recv_sem=receive,
            device_id={"ccd": lax.rem(me + step, count)},
            device_id_type=pl.DeviceIdType.MESH,
        )

    copies = [
        remote(image_ref.at[:, pl.ds(BLOCK - RIM, RIM)], above_ref, rims.at[0], rims.at[1], 1),
        remote(image_ref.at[:, pl.ds(0, RIM)], below_ref, rims.at[2], rims.at[3], count - 1),
    ]
    for step in outward(count):
        copies.append(
            remote(meta_ref, metas_ref.at[me], sent.at[step], received.at[step], step)
        )
    for copy in copies:
        copy.start()
    local = pltpu.make_async_copy(meta_ref, metas_ref.at[me], own)
    local.start()
    local.wait()
    for copy in copies:
        copy.wait()


def trade_kernel(count, send_ref, got_ref, sent, received, own):
    me = lax.axis_index("ccd")
    meet(me, count)
    copies = []
    for step in outward(count):
        peer = lax.rem(me + step, count)
        copies.append(
            pltpu.make_async_remote_copy(
                src_ref=send_ref.at[peer],
                dst_ref=got_ref.at[me],
                send_sem=sent.at[step],
                recv_sem=received.at[step],
                device_id={"ccd": peer},
                device_id_type=pl.DeviceIdType.MESH,
            )
        )
    for copy in copies:
        copy.start()
    local = pltpu.make_async_copy(send_ref.at[me], got_ref.at[me], own)
    local.start()
    local.wait()
    for copy in copies:
        copy.wait()


def split(values):
    high = values.astype(jnp.bfloat16)
    return high, (values - high.astype(jnp.float32)).astype(jnp.bfloat16)


def dot(left, right):
    return jnp.dot(left, right, preferred_element_type=jnp.float32)


def band_kernel(
    devices,
    capacity,
    patch_ref,
    owner_ref,
    taps_ref,
    coef_ref,
    affine_ref,
    above_ref,
    image_ref,
    below_ref,
    send_ref,
    col_high,
    col_low,
    row_kernel,
    wide,
    terms_high,
    terms_low,
    mid,
    target,
    filled,
):
    visit = pl.program_id(0)
    band = lax.axis_index("ccd")
    shifted = band + SPLIT // 2
    ccd = shifted // SPLIT
    top_row = shifted % SPLIT * BLOCK
    region_shift = band * BLOCK - top_row
    region_low = jnp.maximum(0, -region_shift)
    region_high = jnp.minimum(HEIGHT, devices * BLOCK - region_shift)
    ccds = coef_ref.shape[0] // (V * NBASIS * 3)
    place = visit * ccds + ccd
    wide_lane = lax.broadcasted_iota(jnp.int32, (1, NBASIS * ROWS_IN), 1)

    def by_basis(value):
        total = jnp.full((1, NBASIS * ROWS_IN), value(0), jnp.float32)
        for basis in range(1, NBASIS):
            total = jnp.where(wide_lane >= basis * ROWS_IN, value(basis), total)
        return total

    @pl.when(visit == 0)
    def _():
        send_ref[...] = jnp.zeros_like(send_ref)
        for device in range(devices):
            filled[device] = 0
        for block in range(V * BLKC):
            device = owner_ref[patch_ref[block]]
            target[block] = device * capacity + filled[device]
            filled[device] = filled[device] + 1
        depth = lax.broadcasted_iota(jnp.int32, (2 * BLOCK, BLOCK), 0)
        lane = lax.broadcasted_iota(jnp.int32, (2 * BLOCK, BLOCK), 1)
        distance = depth - (LEFT - HALF) - lane
        for basis in range(NBASIS):
            cols = pl.ds(basis * BLOCK, BLOCK)
            total = jnp.zeros((2 * BLOCK, BLOCK), jnp.float32)
            for tap in range(TAPS):
                total = jnp.where(
                    distance == tap, taps_ref[(NBASIS + basis) * TAPS + tap], total
                )
            high, low = split(total)
            col_high[:, cols] = high
            col_low[:, cols] = low
        start = jnp.zeros((1, NBASIS * ROWS_IN), jnp.int32)
        for basis in range(1, NBASIS):
            start = jnp.where(wide_lane >= basis * ROWS_IN, basis * ROWS_IN, start)
        gap = (wide_lane - start) - lax.broadcasted_iota(
            jnp.int32, (ROWS_MID, NBASIS * ROWS_IN), 0
        )
        total = jnp.zeros(gap.shape, jnp.float32)
        for tap in range(TAPS):
            total = jnp.where(
                gap == tap, by_basis(lambda basis: taps_ref[basis * TAPS + tap]), total
            )
        row_kernel[...] = total
        wide[...] = jnp.zeros_like(wide)

    def inside(first, count):
        rows = first + lax.broadcasted_iota(jnp.int32, (count, 1), 0)
        return (rows >= region_low) & (rows < region_high)

    raw = jnp.concatenate([above_ref[0], image_ref[0], below_ref[0]], axis=0)
    raw = jnp.where(inside(top_row - RIM, ROWS_IN), raw, 0.0)
    wide[:, LEFT : LEFT + WIDTH] = raw
    for block in range(BLKC):
        high, low = split(wide[:, block * BLOCK : (block + 2) * BLOCK])
        term = dot(high, col_high[...]) + dot(low, col_high[...]) + dot(high, col_low[...])
        high, low = split(term)
        for basis in range(NBASIS):
            rows = pl.ds(basis * ROWS_IN, ROWS_IN)
            cols = pl.ds(block * BLOCK, BLOCK)
            terms_high[rows, cols] = high[:, basis * BLOCK : (basis + 1) * BLOCK]
            terms_low[rows, cols] = low[:, basis * BLOCK : (basis + 1) * BLOCK]

    position = (top_row - REACH + lax.broadcasted_iota(jnp.int32, (ROWS_MID, 1), 0)).astype(
        jnp.float32
    )
    row_pos = (2.0 * position + 1.0) / HEIGHT - 1.0
    column = lax.broadcasted_iota(jnp.int32, (1, WIDTH), 1).astype(jnp.float32)
    col_pos = (2.0 * column + 1.0) / WIDTH - 1.0
    kernel = row_kernel[...]
    constant, by_row, by_column = (
        by_basis(lambda basis: coef_ref[(place * NBASIS + basis) * 3 + part]) for part in range(3)
    )
    level = kernel * (constant + by_row * row_pos)
    slope = kernel * by_column
    level_high, level_low = split(level)
    slope_high, slope_low = split(slope)
    upper = dot(
        jnp.concatenate([level_high, slope_high, level_low, slope_low], axis=0), terms_high[...]
    )
    lower = dot(jnp.concatenate([level_high, slope_high], axis=0), terms_low[...])
    both = upper[: 2 * ROWS_MID] + upper[2 * ROWS_MID :] + lower
    matched = both[:ROWS_MID] + both[ROWS_MID:] * col_pos
    mid[...] = jnp.where(inside(top_row - REACH, ROWS_MID), matched, 0.0)

    own_rows = (top_row + lax.broadcasted_iota(jnp.int32, (BLOCK, 1), 0)).astype(jnp.float32)
    row_shift = affine_ref[place * 4] + affine_ref[place * 4 + 1] * (
        (own_rows - (HEIGHT - 1) / 2.0) / HEIGHT
    )
    row_step = lax.broadcasted_iota(jnp.int32, (BLOCK, BLOCK), 1) - REACH
    row_weight = lanczos(row_shift - row_step.astype(jnp.float32))
    col_shift = affine_ref[place * 4 + 2] + affine_ref[place * 4 + 3] * (
        (column - (WIDTH - 1) / 2.0) / WIDTH
    )
    col_step = lax.broadcasted_iota(jnp.int32, (8, WIDTH), 0) - REACH
    reached = lax.broadcasted_iota(jnp.int32, (8, WIDTH), 1) + col_step
    col_weight = jnp.where(
        (reached >= 0) & (reached < WIDTH),
        lanczos(col_shift - col_step.astype(jnp.float32)),
        0.0,
    )
    warped = jnp.zeros((BLOCK, WIDTH), jnp.float32)
    for step in range(STEPS):
        warped = warped + row_weight[:, step : step + 1] * mid[step : step + BLOCK, :]
    total = jnp.zeros((BLOCK, WIDTH), jnp.float32)
    for step in range(STEPS):
        offset = step - REACH
        moved = warped if offset == 0 else pltpu.roll(warped, (-offset) % WIDTH, 1)
        total = total + col_weight[step : step + 1, :] * moved
    rounded = total.astype(jnp.bfloat16)
    for block in range(BLKC):
        send_ref[target[visit * BLKC + block]] = rounded[
            :, block * BLOCK : (block + 1) * BLOCK
        ]


def gather_kernel(devices, capacity, meta_ref, owner_ref, weight_ref, got_ref, out_ref, total, weights):
    me = lax.axis_index("ccd")
    total[...] = jnp.zeros_like(total)
    for cell in range(PSIDE * PSIDE):
        weights[cell] = 0.0
    patch = jnp.int32(0)
    for candidate in range(owner_ref.shape[0]):
        patch = jnp.where(owner_ref[candidate] == me, candidate, patch)
    ccds = weight_ref.shape[0] // V
    count = V * BLKC

    def add(source, carry):
        ccd = (source + SPLIT // 2) // SPLIT
        taken = source * capacity
        for block in range(count):
            mine = meta_ref[source, 0, block] == patch

            @pl.when(mine)
            def _(taken=taken, block=block):
                cell = meta_ref[source, 0, count + block]
                weight = weight_ref[block // BLKC * ccds + ccd]
                weights[cell] = weights[cell] + weight
                total[cell] = total[cell] + weight * got_ref[taken].astype(jnp.float32)

            taken = taken + mine.astype(jnp.int32)
        return carry

    lax.fori_loop(0, devices, add, 0)
    for cell in range(PSIDE * PSIDE):
        row, col = cell // PSIDE * BLOCK, cell % PSIDE * BLOCK
        scale = jnp.full((1, BLOCK), jnp.maximum(weights[cell], 1.0), jnp.float32)
        out_ref[0, row : row + BLOCK, col : col + BLOCK] = total[cell] / scale


def shards(
    images, basis_taps, psf_coef, affine, visit_weight, block_patch, block_slot, patch_owner
):
    devices = lax.axis_size("ccd")
    block_count = V * BLKC
    capacity = max(2, (2 * block_count + devices - 1) // devices)
    slots = devices * capacity
    anywhere = pl.BlockSpec(memory_space=pl.ANY)
    scalars = pl.BlockSpec(memory_space=pltpu.SMEM)
    vector = pl.BlockSpec(memory_space=pltpu.VMEM)
    lanes = -(-2 * block_count // BLOCK) * BLOCK
    meta = jnp.pad(
        jnp.concatenate([block_patch[0, :, 0], block_slot[0]]), (0, lanes - 2 * block_count)
    )[None]
    rim_shape = jax.ShapeDtypeStruct((V, RIM, WIDTH), jnp.float32)
    above, below, metas = pl.pallas_call(
        functools.partial(rim_kernel, devices),
        out_shape=(rim_shape, rim_shape, jax.ShapeDtypeStruct((devices, 1, lanes), jnp.int32)),
        in_specs=[anywhere, vector],
        out_specs=(anywhere, anywhere, vector),
        scratch_shapes=[
            pltpu.SemaphoreType.DMA((devices,)),
            pltpu.SemaphoreType.DMA((devices,)),
            pltpu.SemaphoreType.DMA((4,)),
            pltpu.SemaphoreType.DMA,
        ],
        compiler_params=pltpu.CompilerParams(collective_id=1, has_side_effects=True),
    )(images, meta)

    def per_visit(shape):
        return pl.BlockSpec((1,) + shape[1:], lambda v: (v, 0, 0))

    out_shape = (slots, BLOCK, BLOCK)
    send = pl.pallas_call(
        functools.partial(band_kernel, devices, capacity),
        out_shape=jax.ShapeDtypeStruct(out_shape, jnp.bfloat16),
        grid=(V,),
        in_specs=[scalars] * 5
        + [per_visit(above.shape), per_visit(images.shape), per_visit(below.shape)],
        out_specs=pl.BlockSpec(out_shape, lambda v: (0, 0, 0)),
        scratch_shapes=[
            pltpu.VMEM((2 * BLOCK, NBASIS * BLOCK), jnp.bfloat16),
            pltpu.VMEM((2 * BLOCK, NBASIS * BLOCK), jnp.bfloat16),
            pltpu.VMEM((ROWS_MID, NBASIS * ROWS_IN), jnp.float32),
            pltpu.VMEM((ROWS_IN, WIDTH + BLOCK), jnp.float32),
            pltpu.VMEM((NBASIS * ROWS_IN, WIDTH), jnp.bfloat16),
            pltpu.VMEM((NBASIS * ROWS_IN, WIDTH), jnp.bfloat16),
            pltpu.VMEM((ROWS_MID, WIDTH), jnp.float32),
            pltpu.SMEM((block_count,), jnp.int32),
            pltpu.SMEM((devices,), jnp.int32),
        ],
        compiler_params=pltpu.CompilerParams(dimension_semantics=("arbitrary",)),
    )(
        block_patch.reshape(-1),
        patch_owner,
        basis_taps.reshape(-1),
        psf_coef.reshape(-1),
        affine.reshape(-1),
        above,
        images,
        below,
    )
    got = pl.pallas_call(
        functools.partial(trade_kernel, devices),
        out_shape=jax.ShapeDtypeStruct((devices, capacity, BLOCK, BLOCK), jnp.bfloat16),
        in_specs=[anywhere],
        out_specs=anywhere,
        scratch_shapes=[
            pltpu.SemaphoreType.DMA((devices,)),
            pltpu.SemaphoreType.DMA((devices,)),
            pltpu.SemaphoreType.DMA,
        ],
        compiler_params=pltpu.CompilerParams(collective_id=2, has_side_effects=True),
    )(send.reshape(devices, capacity, BLOCK, BLOCK))
    size = PSIDE * BLOCK
    return pl.pallas_call(
        functools.partial(gather_kernel, devices, capacity),
        out_shape=jax.ShapeDtypeStruct((1, size, size), jnp.float32),
        in_specs=[scalars, scalars, scalars, vector],
        out_specs=vector,
        scratch_shapes=[
            pltpu.VMEM((PSIDE * PSIDE, BLOCK, BLOCK), jnp.float32),
            pltpu.SMEM((PSIDE * PSIDE,), jnp.float32),
        ],
    )(metas, patch_owner, visit_weight.astype(jnp.float32).reshape(-1), got.reshape(out_shape))


def solution(mesh):
    placed = (
        P(None, ("group", "ccd"), None),
        P(),
        P(None, "group", None, None),
        P(None, "group", None, None),
        P(None, "group"),
        P(("group", "ccd"), None, None),
        P(("group", "ccd"), None),
        P("group"),
    )
    return jax.shard_map(
        shards,
        mesh=mesh,
        in_specs=placed,
        out_specs=P(("group", "ccd"), None, None),
        check_vma=False,
    )
```

```python
import functools

import jax
import jax.numpy as jnp
from jax import lax
from jax.experimental import pallas as pl
from jax.experimental.pallas import tpu as pltpu
from jax.sharding import PartitionSpec as P

V = 4
BLOCK = 128
BLKC = 4
SPLIT = 4
TAPS = 11
NBASIS = 9
PSIDE = 4
HALF = TAPS // 2
REACH = 3
RIM = HALF + REACH
ROWS_IN = BLOCK + 2 * RIM
ROWS_MID = BLOCK + 8
WIDTH = BLKC * BLOCK
HEIGHT = SPLIT * BLOCK
LEFT = BLOCK // 2
STEPS = 2 * REACH + 1


def sinc(values):
    angle = jnp.pi * values
    zero = values == 0.0
    return jnp.where(zero, 1.0, jnp.sin(angle) / jnp.where(zero, 1.0, angle))


def lanczos(offset):
    inside = jnp.abs(offset) < 3.0
    return jnp.where(inside, sinc(offset) * sinc(offset / 3.0), 0.0)


def outward(count):
    return sorted(range(1, count), key=lambda step: abs(step - count // 2))


def meet(me, count):
    barrier = pltpu.get_barrier_semaphore()
    for step in range(1, count):
        pl.semaphore_signal(
            barrier,
            inc=1,
            device_id={"ccd": lax.rem(me + step, count)},
            device_id_type=pl.DeviceIdType.MESH,
        )
    pl.semaphore_wait(barrier, count - 1)


def rim_kernel(count, image_ref, above_ref, below_ref, rims):
    me = lax.axis_index("ccd")
    barrier = pltpu.get_barrier_semaphore()
    has_next, has_last = me < count - 1, me > 0

    def to_next():
        return pltpu.make_async_remote_copy(
            src_ref=image_ref.at[:, pl.ds(BLOCK - RIM, RIM)],
            dst_ref=above_ref,
            send_sem=rims.at[0],
            recv_sem=rims.at[1],
            device_id={"ccd": lax.rem(me + 1, count)},
            device_id_type=pl.DeviceIdType.MESH,
        )

    def to_last():
        return pltpu.make_async_remote_copy(
            src_ref=image_ref.at[:, pl.ds(0, RIM)],
            dst_ref=below_ref,
            send_sem=rims.at[2],
            recv_sem=rims.at[3],
            device_id={"ccd": lax.rem(me + count - 1, count)},
            device_id_type=pl.DeviceIdType.MESH,
        )

    for present, step in ((has_next, 1), (has_last, count - 1)):

        @pl.when(present)
        def _(step=step):
            pl.semaphore_signal(
                barrier,
                inc=1,
                device_id={"ccd": lax.rem(me + step, count)},
                device_id_type=pl.DeviceIdType.MESH,
            )

    pl.semaphore_wait(barrier, has_next.astype(jnp.int32) + has_last.astype(jnp.int32))

    @pl.when(has_next)
    def _():
        to_next().start()

    @pl.when(has_last)
    def _():
        to_last().start()

    @pl.when(has_next)
    def _():
        to_next().wait_send()
        to_last().wait_recv()

    @pl.when(has_last)
    def _():
        to_last().wait_send()
        to_next().wait_recv()


def trade_kernel(count, meta_ref, send_ref, metas_ref, got_ref, sent, received, own):
    me = lax.axis_index("ccd")
    meet(me, count)
    copies = []
    for step in outward(count):
        peer = lax.rem(me + step, count)
        copies.append(
            pltpu.make_async_remote_copy(
                src_ref=send_ref.at[peer],
                dst_ref=got_ref.at[me],
                send_sem=sent.at[0, step],
                recv_sem=received.at[0, step],
                device_id={"ccd": peer},
                device_id_type=pl.DeviceIdType.MESH,
            )
        )
    for step in outward(count):
        copies.append(
            pltpu.make_async_remote_copy(
                src_ref=meta_ref,
                dst_ref=metas_ref.at[me],
                send_sem=sent.at[1, step],
                recv_sem=received.at[1, step],
                device_id={"ccd": lax.rem(me + step, count)},
                device_id_type=pl.DeviceIdType.MESH,
            )
        )
    for copy in copies:
        copy.start()
    own_blocks = pltpu.make_async_copy(send_ref.at[me], got_ref.at[me], own.at[0])
    own_meta = pltpu.make_async_copy(meta_ref, metas_ref.at[me], own.at[1])
    own_blocks.start()
    own_meta.start()
    own_blocks.wait()
    own_meta.wait()
    for copy in copies:
        copy.wait()


def split(values):
    high = values.astype(jnp.bfloat16)
    return high, (values - high.astype(jnp.float32)).astype(jnp.bfloat16)


def dot(left, right):
    return jnp.dot(left, right, preferred_element_type=jnp.float32)


def band_kernel(
    devices,
    capacity,
    patch_ref,
    owner_ref,
    taps_ref,
    coef_ref,
    affine_ref,
    above_ref,
    image_ref,
    below_ref,
    send_ref,
    col_high,
    col_low,
    row_kernel,
    wide,
    terms_high,
    terms_low,
    mid,
    target,
    filled,
):
    visit = pl.program_id(0)
    band = lax.axis_index("ccd")
    shifted = band + SPLIT // 2
    ccd = shifted // SPLIT
    top_row = shifted % SPLIT * BLOCK
    region_shift = band * BLOCK - top_row
    region_low = jnp.maximum(0, -region_shift)
    region_high = jnp.minimum(HEIGHT, devices * BLOCK - region_shift)
    ccds = coef_ref.shape[0] // (V * NBASIS * 3)
    place = visit * ccds + ccd
    wide_lane = lax.broadcasted_iota(jnp.int32, (1, NBASIS * ROWS_IN), 1)

    def by_basis(value):
        total = jnp.full((1, NBASIS * ROWS_IN), value(0), jnp.float32)
        for basis in range(1, NBASIS):
            total = jnp.where(wide_lane >= basis * ROWS_IN, value(basis), total)
        return total

    @pl.when(visit == 0)
    def _():
        send_ref[...] = jnp.zeros_like(send_ref)
        for device in range(devices):
            filled[device] = 0
        for block in range(V * BLKC):
            device = owner_ref[patch_ref[block]]
            target[block] = device * capacity + filled[device]
            filled[device] = filled[device] + 1
        depth = lax.broadcasted_iota(jnp.int32, (2 * BLOCK, BLOCK), 0)
        lane = lax.broadcasted_iota(jnp.int32, (2 * BLOCK, BLOCK), 1)
        distance = depth - (LEFT - HALF) - lane
        for basis in range(NBASIS):
            cols = pl.ds(basis * BLOCK, BLOCK)
            total = jnp.zeros((2 * BLOCK, BLOCK), jnp.float32)
            for tap in range(TAPS):
                total = jnp.where(
                    distance == tap, taps_ref[(NBASIS + basis) * TAPS + tap], total
                )
            high, low = split(total)
            col_high[:, cols] = high
            col_low[:, cols] = low
        start = jnp.zeros((1, NBASIS * ROWS_IN), jnp.int32)
        for basis in range(1, NBASIS):
            start = jnp.where(wide_lane >= basis * ROWS_IN, basis * ROWS_IN, start)
        gap = (wide_lane - start) - lax.broadcasted_iota(
            jnp.int32, (ROWS_MID, NBASIS * ROWS_IN), 0
        )
        total = jnp.zeros(gap.shape, jnp.float32)
        for tap in range(TAPS):
            total = jnp.where(
                gap == tap, by_basis(lambda basis: taps_ref[basis * TAPS + tap]), total
            )
        row_kernel[...] = total
        wide[...] = jnp.zeros_like(wide)

    def inside(first, count):
        rows = first + lax.broadcasted_iota(jnp.int32, (count, 1), 0)
        return (rows >= region_low) & (rows < region_high)

    raw = jnp.concatenate([above_ref[0], image_ref[0], below_ref[0]], axis=0)
    raw = jnp.where(inside(top_row - RIM, ROWS_IN), raw, 0.0)
    wide[:, LEFT : LEFT + WIDTH] = raw
    for block in range(BLKC):
        high, low = split(wide[:, block * BLOCK : (block + 2) * BLOCK])
        term = dot(high, col_high[...]) + dot(low, col_high[...]) + dot(high, col_low[...])
        high, low = split(term)
        for basis in range(NBASIS):
            rows = pl.ds(basis * ROWS_IN, ROWS_IN)
            cols = pl.ds(block * BLOCK, BLOCK)
            terms_high[rows, cols] = high[:, basis * BLOCK : (basis + 1) * BLOCK]
            terms_low[rows, cols] = low[:, basis * BLOCK : (basis + 1) * BLOCK]

    position = (top_row - REACH + lax.broadcasted_iota(jnp.int32, (ROWS_MID, 1), 0)).astype(
        jnp.float32
    )
    row_pos = (2.0 * position + 1.0) / HEIGHT - 1.0
    column = lax.broadcasted_iota(jnp.int32, (1, WIDTH), 1).astype(jnp.float32)
    col_pos = (2.0 * column + 1.0) / WIDTH - 1.0
    kernel = row_kernel[...]
    constant, by_row, by_column = (
        by_basis(lambda basis: coef_ref[(place * NBASIS + basis) * 3 + part]) for part in range(3)
    )
    level = kernel * (constant + by_row * row_pos)
    slope = kernel * by_column
    level_high, level_low = split(level)
    slope_high, slope_low = split(slope)
    upper = dot(
        jnp.concatenate([level_high, slope_high, level_low, slope_low], axis=0), terms_high[...]
    )
    lower = dot(jnp.concatenate([level_high, slope_high], axis=0), terms_low[...])
    both = upper[: 2 * ROWS_MID] + upper[2 * ROWS_MID :] + lower
    matched = both[:ROWS_MID] + both[ROWS_MID:] * col_pos
    mid[...] = jnp.where(inside(top_row - REACH, ROWS_MID), matched, 0.0)

    own_rows = (top_row + lax.broadcasted_iota(jnp.int32, (BLOCK, 1), 0)).astype(jnp.float32)
    row_shift = affine_ref[place * 4] + affine_ref[place * 4 + 1] * (
        (own_rows - (HEIGHT - 1) / 2.0) / HEIGHT
    )
    row_step = lax.broadcasted_iota(jnp.int32, (BLOCK, BLOCK), 1) - REACH
    row_weight = lanczos(row_shift - row_step.astype(jnp.float32))
    col_shift = affine_ref[place * 4 + 2] + affine_ref[place * 4 + 3] * (
        (column - (WIDTH - 1) / 2.0) / WIDTH
    )
    col_step = lax.broadcasted_iota(jnp.int32, (8, WIDTH), 0) - REACH
    reached = lax.broadcasted_iota(jnp.int32, (8, WIDTH), 1) + col_step
    col_weight = jnp.where(
        (reached >= 0) & (reached < WIDTH),
        lanczos(col_shift - col_step.astype(jnp.float32)),
        0.0,
    )
    warped = jnp.zeros((BLOCK, WIDTH), jnp.float32)
    for step in range(STEPS):
        warped = warped + row_weight[:, step : step + 1] * mid[step : step + BLOCK, :]
    total = jnp.zeros((BLOCK, WIDTH), jnp.float32)
    for step in range(STEPS):
        offset = step - REACH
        moved = warped if offset == 0 else pltpu.roll(warped, (-offset) % WIDTH, 1)
        total = total + col_weight[step : step + 1, :] * moved
    rounded = total.astype(jnp.bfloat16)
    for block in range(BLKC):
        send_ref[target[visit * BLKC + block]] = rounded[
            :, block * BLOCK : (block + 1) * BLOCK
        ]


def gather_kernel(devices, capacity, meta_ref, owner_ref, weight_ref, got_ref, out_ref, total, weights):
    me = lax.axis_index("ccd")
    total[...] = jnp.zeros_like(total)
    for cell in range(PSIDE * PSIDE):
        weights[cell] = 0.0
    patch = jnp.int32(0)
    for candidate in range(owner_ref.shape[0]):
        patch = jnp.where(owner_ref[candidate] == me, candidate, patch)
    ccds = weight_ref.shape[0] // V
    count = V * BLKC

    def add(source, carry):
        ccd = (source + SPLIT // 2) // SPLIT
        taken = source * capacity
        for block in range(count):
            mine = meta_ref[source, 0, block] == patch

            @pl.when(mine)
            def _(taken=taken, block=block):
                cell = meta_ref[source, 0, count + block]
                weight = weight_ref[block // BLKC * ccds + ccd]
                weights[cell] = weights[cell] + weight
                total[cell] = total[cell] + weight * got_ref[taken].astype(jnp.float32)

            taken = taken + mine.astype(jnp.int32)
        return carry

    lax.fori_loop(0, devices, add, 0)
    for cell in range(PSIDE * PSIDE):
        row, col = cell // PSIDE * BLOCK, cell % PSIDE * BLOCK
        scale = jnp.full((1, BLOCK), jnp.maximum(weights[cell], 1.0), jnp.float32)
        out_ref[0, row : row + BLOCK, col : col + BLOCK] = total[cell] / scale


def shards(
    images, basis_taps, psf_coef, affine, visit_weight, block_patch, block_slot, patch_owner
):
    devices = lax.axis_size("ccd")
    block_count = V * BLKC
    capacity = max(2, (2 * block_count + devices - 1) // devices)
    slots = devices * capacity
    anywhere = pl.BlockSpec(memory_space=pl.ANY)
    scalars = pl.BlockSpec(memory_space=pltpu.SMEM)
    vector = pl.BlockSpec(memory_space=pltpu.VMEM)
    lanes = -(-2 * block_count // BLOCK) * BLOCK
    meta = jnp.pad(
        jnp.concatenate([block_patch[0, :, 0], block_slot[0]]), (0, lanes - 2 * block_count)
    )[None]
    rim_shape = jax.ShapeDtypeStruct((V, RIM, WIDTH), jnp.float32)
    above, below = pl.pallas_call(
        functools.partial(rim_kernel, devices),
        out_shape=(rim_shape, rim_shape),
        in_specs=[anywhere],
        out_specs=(anywhere, anywhere),
        scratch_shapes=[pltpu.SemaphoreType.DMA((4,))],
        compiler_params=pltpu.CompilerParams(collective_id=1, has_side_effects=True),
    )(images)

    def per_visit(shape):
        return pl.BlockSpec((1,) + shape[1:], lambda v: (v, 0, 0))

    out_shape = (slots, BLOCK, BLOCK)
    send = pl.pallas_call(
        functools.partial(band_kernel, devices, capacity),
        out_shape=jax.ShapeDtypeStruct(out_shape, jnp.bfloat16),
        grid=(V,),
        in_specs=[scalars] * 5
        + [per_visit(above.shape), per_visit(images.shape), per_visit(below.shape)],
        out_specs=pl.BlockSpec(out_shape, lambda v: (0, 0, 0)),
        scratch_shapes=[
            pltpu.VMEM((2 * BLOCK, NBASIS * BLOCK), jnp.bfloat16),
            pltpu.VMEM((2 * BLOCK, NBASIS * BLOCK), jnp.bfloat16),
            pltpu.VMEM((ROWS_MID, NBASIS * ROWS_IN), jnp.float32),
            pltpu.VMEM((ROWS_IN, WIDTH + BLOCK), jnp.float32),
            pltpu.VMEM((NBASIS * ROWS_IN, WIDTH), jnp.bfloat16),
            pltpu.VMEM((NBASIS * ROWS_IN, WIDTH), jnp.bfloat16),
            pltpu.VMEM((ROWS_MID, WIDTH), jnp.float32),
            pltpu.SMEM((block_count,), jnp.int32),
            pltpu.SMEM((devices,), jnp.int32),
        ],
        compiler_params=pltpu.CompilerParams(dimension_semantics=("arbitrary",)),
    )(
        block_patch.reshape(-1),
        patch_owner,
        basis_taps.reshape(-1),
        psf_coef.reshape(-1),
        affine.reshape(-1),
        above,
        images,
        below,
    )
    metas, got = pl.pallas_call(
        functools.partial(trade_kernel, devices),
        out_shape=(
            jax.ShapeDtypeStruct((devices, 1, lanes), jnp.int32),
            jax.ShapeDtypeStruct((devices, capacity, BLOCK, BLOCK), jnp.bfloat16),
        ),
        in_specs=[vector, anywhere],
        out_specs=(vector, anywhere),
        scratch_shapes=[
            pltpu.SemaphoreType.DMA((2, devices)),
            pltpu.SemaphoreType.DMA((2, devices)),
            pltpu.SemaphoreType.DMA((2,)),
        ],
        compiler_params=pltpu.CompilerParams(collective_id=2, has_side_effects=True),
    )(meta, send.reshape(devices, capacity, BLOCK, BLOCK))
    size = PSIDE * BLOCK
    return pl.pallas_call(
        functools.partial(gather_kernel, devices, capacity),
        out_shape=jax.ShapeDtypeStruct((1, size, size), jnp.float32),
        in_specs=[scalars, scalars, scalars, vector],
        out_specs=vector,
        scratch_shapes=[
            pltpu.VMEM((PSIDE * PSIDE, BLOCK, BLOCK), jnp.float32),
            pltpu.SMEM((PSIDE * PSIDE,), jnp.float32),
        ],
    )(metas, patch_owner, visit_weight.astype(jnp.float32).reshape(-1), got.reshape(out_shape))


def solution(mesh):
    placed = (
        P(None, ("group", "ccd"), None),
        P(),
        P(None, "group", None, None),
        P(None, "group", None, None),
        P(None, "group"),
        P(("group", "ccd"), None, None),
        P(("group", "ccd"), None),
        P("group"),
    )
    return jax.shard_map(
        shards,
        mesh=mesh,
        in_specs=placed,
        out_specs=P(("group", "ccd"), None, None),
        check_vma=False,
    )
```

```python
import functools

import jax
import jax.numpy as jnp
from jax import lax
from jax.experimental import pallas as pl
from jax.experimental.pallas import tpu as pltpu
from jax.sharding import PartitionSpec as P

V = 4
BLOCK = 128
BLKC = 4
SPLIT = 4
TAPS = 11
NBASIS = 9
PSIDE = 4
HALF = TAPS // 2
REACH = 3
RIM = HALF + REACH
CHUNKS = 2
CHUNK = BLOCK // CHUNKS
ROWS_IN = CHUNK + 2 * RIM
ROWS_MID = CHUNK + 8
WIDTH = BLKC * BLOCK
HEIGHT = SPLIT * BLOCK
LEFT = BLOCK // 2
STEPS = 2 * REACH + 1


def sinc(values):
    angle = jnp.pi * values
    zero = values == 0.0
    return jnp.where(zero, 1.0, jnp.sin(angle) / jnp.where(zero, 1.0, angle))


def lanczos(offset):
    inside = jnp.abs(offset) < 3.0
    return jnp.where(inside, sinc(offset) * sinc(offset / 3.0), 0.0)


def outward(count):
    return sorted(range(1, count), key=lambda step: abs(step - count // 2))


def rim_kernel(count, image_ref, above_ref, below_ref, rims):
    me = lax.axis_index("ccd")
    barrier = pltpu.get_barrier_semaphore()
    has_next, has_last = me < count - 1, me > 0

    def to_next():
        return pltpu.make_async_remote_copy(
            src_ref=image_ref.at[:, pl.ds(BLOCK - RIM, RIM)],
            dst_ref=above_ref,
            send_sem=rims.at[0],
            recv_sem=rims.at[1],
            device_id={"ccd": lax.rem(me + 1, count)},
            device_id_type=pl.DeviceIdType.MESH,
        )

    def to_last():
        return pltpu.make_async_remote_copy(
            src_ref=image_ref.at[:, pl.ds(0, RIM)],
            dst_ref=below_ref,
            send_sem=rims.at[2],
            recv_sem=rims.at[3],
            device_id={"ccd": lax.rem(me + count - 1, count)},
            device_id_type=pl.DeviceIdType.MESH,
        )

    for present, step in ((has_next, 1), (has_last, count - 1)):

        @pl.when(present)
        def _(step=step):
            pl.semaphore_signal(
                barrier,
                inc=1,
                device_id={"ccd": lax.rem(me + step, count)},
                device_id_type=pl.DeviceIdType.MESH,
            )

    pl.semaphore_wait(barrier, has_next.astype(jnp.int32) + has_last.astype(jnp.int32))

    @pl.when(has_next)
    def _():
        to_next().start()

    @pl.when(has_last)
    def _():
        to_last().start()

    @pl.when(has_next)
    def _():
        to_next().wait_send()
        to_last().wait_recv()

    @pl.when(has_last)
    def _():
        to_last().wait_send()
        to_next().wait_recv()


def split(values):
    high = values.astype(jnp.bfloat16)
    return high, (values - high.astype(jnp.float32)).astype(jnp.bfloat16)


def dot(left, right):
    return jnp.dot(left, right, preferred_element_type=jnp.float32)


def plan_kernel(devices, capacity, patch_ref, owner_ref, block_ref, filled):
    for device in range(devices):
        filled[device] = 0
    for slot in range(devices * capacity):
        block_ref[slot] = 0
    for block in range(V * BLKC):
        device = owner_ref[patch_ref[block]]
        block_ref[device * capacity + filled[device]] = block
        filled[device] = filled[device] + 1


def band_kernel(
    devices,
    capacity,
    block_ref,
    taps_ref,
    coef_ref,
    affine_ref,
    meta_ref,
    above_ref,
    image_ref,
    below_ref,
    metas_ref,
    got_ref,
    col_high,
    col_low,
    row_kernel,
    wide,
    terms_high,
    terms_low,
    mid,
    stage,
    outbox,
    sent,
    received,
    own,
):
    band = lax.axis_index("ccd")
    barrier = pltpu.get_barrier_semaphore()
    for step in range(1, devices):
        pl.semaphore_signal(
            barrier,
            inc=1,
            device_id={"ccd": lax.rem(band + step, devices)},
            device_id_type=pl.DeviceIdType.MESH,
        )
    shifted = band + SPLIT // 2
    ccd = shifted // SPLIT
    top_row = shifted % SPLIT * BLOCK
    region_shift = band * BLOCK - top_row
    region_low = jnp.maximum(0, -region_shift)
    region_high = jnp.minimum(HEIGHT, devices * BLOCK - region_shift)
    ccds = coef_ref.shape[0] // (V * NBASIS * 3)
    wide_lane = lax.broadcasted_iota(jnp.int32, (1, NBASIS * ROWS_IN), 1)

    def by_basis(value):
        total = jnp.full((1, NBASIS * ROWS_IN), value(0), jnp.float32)
        for basis in range(1, NBASIS):
            total = jnp.where(wide_lane >= basis * ROWS_IN, value(basis), total)
        return total

    def inside(first, count):
        rows = first + lax.broadcasted_iota(jnp.int32, (count, 1), 0)
        return (rows >= region_low) & (rows < region_high)

    depth = lax.broadcasted_iota(jnp.int32, (2 * BLOCK, BLOCK), 0)
    lane = lax.broadcasted_iota(jnp.int32, (2 * BLOCK, BLOCK), 1)
    distance = depth - (LEFT - HALF) - lane
    for basis in range(NBASIS):
        cols = pl.ds(basis * BLOCK, BLOCK)
        total = jnp.zeros((2 * BLOCK, BLOCK), jnp.float32)
        for tap in range(TAPS):
            total = jnp.where(
                distance == tap, taps_ref[(NBASIS + basis) * TAPS + tap], total
            )
        high, low = split(total)
        col_high[:, cols] = high
        col_low[:, cols] = low
    start = jnp.zeros((1, NBASIS * ROWS_IN), jnp.int32)
    for basis in range(1, NBASIS):
        start = jnp.where(wide_lane >= basis * ROWS_IN, basis * ROWS_IN, start)
    gap = (wide_lane - start) - lax.broadcasted_iota(
        jnp.int32, (ROWS_MID, NBASIS * ROWS_IN), 0
    )
    total = jnp.zeros(gap.shape, jnp.float32)
    for tap in range(TAPS):
        total = jnp.where(
            gap == tap, by_basis(lambda basis: taps_ref[basis * TAPS + tap]), total
        )
    row_kernel[...] = total
    wide[...] = jnp.zeros_like(wide)

    column = lax.broadcasted_iota(jnp.int32, (1, WIDTH), 1).astype(jnp.float32)
    col_pos = (2.0 * column + 1.0) / WIDTH - 1.0

    def remote(source, target, kind, step):
        return pltpu.make_async_remote_copy(
            src_ref=source,
            dst_ref=target,
            send_sem=sent.at[kind, step],
            recv_sem=received.at[kind, step],
            device_id={"ccd": lax.rem(band + step, devices)},
            device_id_type=pl.DeviceIdType.MESH,
        )

    pl.semaphore_wait(barrier, devices - 1)
    copies = [
        remote(meta_ref, metas_ref.at[band], CHUNKS, step) for step in outward(devices)
    ]
    locals_ = [pltpu.make_async_copy(meta_ref, metas_ref.at[band], own.at[CHUNKS])]
    for copy in copies + locals_:
        copy.start()
    for chunk in range(CHUNKS):
        first = top_row + chunk * CHUNK

        def one_visit(visit, carry, chunk=chunk, first=first):
            place = visit * ccds + ccd
            raw = jnp.concatenate([above_ref[visit], image_ref[visit], below_ref[visit]], axis=0)
            raw = raw[chunk * CHUNK : chunk * CHUNK + ROWS_IN]
            raw = jnp.where(inside(first - RIM, ROWS_IN), raw, 0.0)
            wide[:, LEFT : LEFT + WIDTH] = raw
            for block in range(BLKC):
                high, low = split(wide[:, block * BLOCK : (block + 2) * BLOCK])
                term = dot(high, col_high[...]) + dot(low, col_high[...]) + dot(high, col_low[...])
                high, low = split(term)
                for basis in range(NBASIS):
                    rows = pl.ds(basis * ROWS_IN, ROWS_IN)
                    cols = pl.ds(block * BLOCK, BLOCK)
                    terms_high[rows, cols] = high[:, basis * BLOCK : (basis + 1) * BLOCK]
                    terms_low[rows, cols] = low[:, basis * BLOCK : (basis + 1) * BLOCK]

            position = (first - REACH + lax.broadcasted_iota(jnp.int32, (ROWS_MID, 1), 0)).astype(
                jnp.float32
            )
            row_pos = (2.0 * position + 1.0) / HEIGHT - 1.0
            kernel = row_kernel[...]
            constant, by_row, by_column = (
                by_basis(lambda basis: coef_ref[(place * NBASIS + basis) * 3 + part]) for part in range(3)
            )
            level = kernel * (constant + by_row * row_pos)
            slope = kernel * by_column
            level_high, level_low = split(level)
            slope_high, slope_low = split(slope)
            upper = dot(
                jnp.concatenate([level_high, slope_high, level_low, slope_low], axis=0), terms_high[...]
            )
            lower = dot(jnp.concatenate([level_high, slope_high], axis=0), terms_low[...])
            both = upper[: 2 * ROWS_MID] + upper[2 * ROWS_MID :] + lower
            matched = both[:ROWS_MID] + both[ROWS_MID:] * col_pos
            mid[...] = jnp.where(inside(first - REACH, ROWS_MID), matched, 0.0)

            own_rows = (first + lax.broadcasted_iota(jnp.int32, (CHUNK, 1), 0)).astype(jnp.float32)
            row_shift = affine_ref[place * 4] + affine_ref[place * 4 + 1] * (
                (own_rows - (HEIGHT - 1) / 2.0) / HEIGHT
            )
            row_step = lax.broadcasted_iota(jnp.int32, (CHUNK, BLOCK), 1) - REACH
            row_weight = lanczos(row_shift - row_step.astype(jnp.float32))
            col_shift = affine_ref[place * 4 + 2] + affine_ref[place * 4 + 3] * (
                (column - (WIDTH - 1) / 2.0) / WIDTH
            )
            col_step = lax.broadcasted_iota(jnp.int32, (8, WIDTH), 0) - REACH
            reached = lax.broadcasted_iota(jnp.int32, (8, WIDTH), 1) + col_step
            col_weight = jnp.where(
                (reached >= 0) & (reached < WIDTH),
                lanczos(col_shift - col_step.astype(jnp.float32)),
                0.0,
            )
            warped = jnp.zeros((CHUNK, WIDTH), jnp.float32)
            for step in range(STEPS):
                warped = warped + row_weight[:, step : step + 1] * mid[step : step + CHUNK, :]
            total = jnp.zeros((CHUNK, WIDTH), jnp.float32)
            for step in range(STEPS):
                offset = step - REACH
                moved = warped if offset == 0 else pltpu.roll(warped, (-offset) % WIDTH, 1)
                total = total + col_weight[step : step + 1, :] * moved
            rounded = total.astype(jnp.bfloat16)
            for block in range(BLKC):
                stage[chunk * V * BLKC + visit * BLKC + block] = rounded[
                    :, block * BLOCK : (block + 1) * BLOCK
                ]
            return carry

        lax.fori_loop(0, V, one_visit, 0)
        for device in range(devices):
            for slot in range(capacity):
                outbox[chunk, device, slot] = stage[
                    chunk * V * BLKC + block_ref[device * capacity + slot]
                ]
        batch = [
            remote(
                outbox.at[chunk, lax.rem(band + step, devices)],
                got_ref.at[chunk, band],
                chunk,
                step,
            )
            for step in outward(devices)
        ]
        local = pltpu.make_async_copy(
            outbox.at[chunk, band], got_ref.at[chunk, band], own.at[chunk]
        )
        for copy in batch + [local]:
            copy.start()
        copies += batch
        locals_.append(local)
    for copy in locals_ + copies:
        copy.wait()


def gather_kernel(devices, capacity, meta_ref, owner_ref, weight_ref, got_ref, out_ref, total, weights):
    me = lax.axis_index("ccd")
    total[...] = jnp.zeros_like(total)
    for cell in range(PSIDE * PSIDE):
        weights[cell] = 0.0
    patch = jnp.int32(0)
    for candidate in range(owner_ref.shape[0]):
        patch = jnp.where(owner_ref[candidate] == me, candidate, patch)
    ccds = weight_ref.shape[0] // V
    count = V * BLKC

    def add(source, carry):
        ccd = (source + SPLIT // 2) // SPLIT
        taken = source * capacity
        for block in range(count):
            mine = meta_ref[source, 0, block] == patch

            @pl.when(mine)
            def _(taken=taken, block=block):
                cell = meta_ref[source, 0, count + block]
                weight = weight_ref[block // BLKC * ccds + ccd]
                weights[cell] = weights[cell] + weight
                for chunk in range(CHUNKS):
                    rows = pl.ds(chunk * CHUNK, CHUNK)
                    total[cell, rows] = total[cell, rows] + weight * got_ref[
                        chunk, taken
                    ].astype(jnp.float32)

            taken = taken + mine.astype(jnp.int32)
        return carry

    lax.fori_loop(0, devices, add, 0)
    for cell in range(PSIDE * PSIDE):
        row, col = cell // PSIDE * BLOCK, cell % PSIDE * BLOCK
        scale = jnp.full((1, BLOCK), jnp.maximum(weights[cell], 1.0), jnp.float32)
        out_ref[0, row : row + BLOCK, col : col + BLOCK] = total[cell] / scale


def shards(
    images, basis_taps, psf_coef, affine, visit_weight, block_patch, block_slot, patch_owner
):
    devices = lax.axis_size("ccd")
    block_count = V * BLKC
    capacity = max(2, (2 * block_count + devices - 1) // devices)
    slots = devices * capacity
    anywhere = pl.BlockSpec(memory_space=pl.ANY)
    scalars = pl.BlockSpec(memory_space=pltpu.SMEM)
    vector = pl.BlockSpec(memory_space=pltpu.VMEM)
    lanes = -(-2 * block_count // BLOCK) * BLOCK
    meta = jnp.pad(
        jnp.concatenate([block_patch[0, :, 0], block_slot[0]]), (0, lanes - 2 * block_count)
    )[None]
    rim_shape = jax.ShapeDtypeStruct((V, RIM, WIDTH), jnp.float32)
    above, below = pl.pallas_call(
        functools.partial(rim_kernel, devices),
        out_shape=(rim_shape, rim_shape),
        in_specs=[anywhere],
        out_specs=(anywhere, anywhere),
        scratch_shapes=[pltpu.SemaphoreType.DMA((4,))],
        compiler_params=pltpu.CompilerParams(collective_id=1, has_side_effects=True),
    )(images)

    blocks = pl.pallas_call(
        functools.partial(plan_kernel, devices, capacity),
        out_shape=jax.ShapeDtypeStruct((slots,), jnp.int32),
        in_specs=[scalars, scalars],
        out_specs=scalars,
        scratch_shapes=[pltpu.SMEM((devices,), jnp.int32)],
    )(block_patch.reshape(-1), patch_owner)
    metas, got = pl.pallas_call(
        functools.partial(band_kernel, devices, capacity),
        out_shape=(
            jax.ShapeDtypeStruct((devices, 1, lanes), jnp.int32),
            jax.ShapeDtypeStruct((CHUNKS, devices, capacity, CHUNK, BLOCK), jnp.bfloat16),
        ),
        in_specs=[scalars] * 4 + [vector] * 4,
        out_specs=(vector, anywhere),
        scratch_shapes=[
            pltpu.VMEM((2 * BLOCK, NBASIS * BLOCK), jnp.bfloat16),
            pltpu.VMEM((2 * BLOCK, NBASIS * BLOCK), jnp.bfloat16),
            pltpu.VMEM((ROWS_MID, NBASIS * ROWS_IN), jnp.float32),
            pltpu.VMEM((ROWS_IN, WIDTH + BLOCK), jnp.float32),
            pltpu.VMEM((NBASIS * ROWS_IN, WIDTH), jnp.bfloat16),
            pltpu.VMEM((NBASIS * ROWS_IN, WIDTH), jnp.bfloat16),
            pltpu.VMEM((ROWS_MID, WIDTH), jnp.float32),
            pltpu.VMEM((CHUNKS * block_count, CHUNK, BLOCK), jnp.bfloat16),
            pltpu.VMEM((CHUNKS, devices, capacity, CHUNK, BLOCK), jnp.bfloat16),
            pltpu.SemaphoreType.DMA((CHUNKS + 1, devices)),
            pltpu.SemaphoreType.DMA((CHUNKS + 1, devices)),
            pltpu.SemaphoreType.DMA((CHUNKS + 1,)),
        ],
        compiler_params=pltpu.CompilerParams(collective_id=2, has_side_effects=True),
    )(
        blocks,
        basis_taps.reshape(-1),
        psf_coef.reshape(-1),
        affine.reshape(-1),
        meta,
        above,
        images,
        below,
    )
    size = PSIDE * BLOCK
    return pl.pallas_call(
        functools.partial(gather_kernel, devices, capacity),
        out_shape=jax.ShapeDtypeStruct((1, size, size), jnp.float32),
        in_specs=[scalars, scalars, scalars, vector],
        out_specs=vector,
        scratch_shapes=[
            pltpu.VMEM((PSIDE * PSIDE, BLOCK, BLOCK), jnp.float32),
            pltpu.SMEM((PSIDE * PSIDE,), jnp.float32),
        ],
    )(metas, patch_owner, visit_weight.astype(jnp.float32).reshape(-1), got.reshape(CHUNKS, slots, CHUNK, BLOCK))


def solution(mesh):
    placed = (
        P(None, ("group", "ccd"), None),
        P(),
        P(None, "group", None, None),
        P(None, "group", None, None),
        P(None, "group"),
        P(("group", "ccd"), None, None),
        P(("group", "ccd"), None),
        P("group"),
    )
    return jax.shard_map(
        shards,
        mesh=mesh,
        in_specs=placed,
        out_specs=P(("group", "ccd"), None, None),
        check_vma=False,
    )
```

```python
import functools

import jax
import jax.numpy as jnp
from jax import lax
from jax.experimental import pallas as pl
from jax.experimental.pallas import tpu as pltpu
from jax.sharding import PartitionSpec as P

V = 4
BLOCK = 128
BLKC = 4
SPLIT = 4
TAPS = 11
NBASIS = 9
PSIDE = 4
HALF = TAPS // 2
REACH = 3
RIM = HALF + REACH
CHUNKS = 4
CHUNK = BLOCK // CHUNKS
ROWS_IN = CHUNK + 2 * RIM
ROWS_MID = CHUNK + 8
WIDTH = BLKC * BLOCK
HEIGHT = SPLIT * BLOCK
LEFT = BLOCK // 2
STEPS = 2 * REACH + 1


def sinc(values):
    angle = jnp.pi * values
    zero = values == 0.0
    return jnp.where(zero, 1.0, jnp.sin(angle) / jnp.where(zero, 1.0, angle))


def lanczos(offset):
    inside = jnp.abs(offset) < 3.0
    return jnp.where(inside, sinc(offset) * sinc(offset / 3.0), 0.0)


def outward(count):
    return sorted(range(1, count), key=lambda step: abs(step - count // 2))


def rim_kernel(count, image_ref, above_ref, below_ref, rims):
    me = lax.axis_index("ccd")
    barrier = pltpu.get_barrier_semaphore()
    has_next, has_last = me < count - 1, me > 0

    def to_next():
        return pltpu.make_async_remote_copy(
            src_ref=image_ref.at[:, pl.ds(BLOCK - RIM, RIM)],
            dst_ref=above_ref,
            send_sem=rims.at[0],
            recv_sem=rims.at[1],
            device_id={"ccd": lax.rem(me + 1, count)},
            device_id_type=pl.DeviceIdType.MESH,
        )

    def to_last():
        return pltpu.make_async_remote_copy(
            src_ref=image_ref.at[:, pl.ds(0, RIM)],
            dst_ref=below_ref,
            send_sem=rims.at[2],
            recv_sem=rims.at[3],
            device_id={"ccd": lax.rem(me + count - 1, count)},
            device_id_type=pl.DeviceIdType.MESH,
        )

    for present, step in ((has_next, 1), (has_last, count - 1)):

        @pl.when(present)
        def _(step=step):
            pl.semaphore_signal(
                barrier,
                inc=1,
                device_id={"ccd": lax.rem(me + step, count)},
                device_id_type=pl.DeviceIdType.MESH,
            )

    pl.semaphore_wait(barrier, has_next.astype(jnp.int32) + has_last.astype(jnp.int32))

    @pl.when(has_next)
    def _():
        to_next().start()

    @pl.when(has_last)
    def _():
        to_last().start()

    @pl.when(has_next)
    def _():
        to_next().wait_send()
        to_last().wait_recv()

    @pl.when(has_last)
    def _():
        to_last().wait_send()
        to_next().wait_recv()


def split(values):
    high = values.astype(jnp.bfloat16)
    return high, (values - high.astype(jnp.float32)).astype(jnp.bfloat16)


def dot(left, right):
    return jnp.dot(left, right, preferred_element_type=jnp.float32)


def plan_kernel(devices, capacity, patch_ref, owner_ref, block_ref, filled):
    for device in range(devices):
        filled[device] = 0
    for slot in range(devices * capacity):
        block_ref[slot] = 0
    for block in range(V * BLKC):
        device = owner_ref[patch_ref[block]]
        block_ref[device * capacity + filled[device]] = block
        filled[device] = filled[device] + 1


def band_kernel(
    devices,
    capacity,
    block_ref,
    taps_ref,
    coef_ref,
    affine_ref,
    meta_ref,
    above_ref,
    image_ref,
    below_ref,
    metas_ref,
    got_ref,
    col_high,
    col_low,
    row_kernel,
    wide,
    terms_high,
    terms_low,
    mid,
    stage,
    outbox,
    sent,
    received,
    own,
):
    band = lax.axis_index("ccd")
    barrier = pltpu.get_barrier_semaphore()
    for step in range(1, devices):
        pl.semaphore_signal(
            barrier,
            inc=1,
            device_id={"ccd": lax.rem(band + step, devices)},
            device_id_type=pl.DeviceIdType.MESH,
        )
    shifted = band + SPLIT // 2
    ccd = shifted // SPLIT
    top_row = shifted % SPLIT * BLOCK
    region_shift = band * BLOCK - top_row
    region_low = jnp.maximum(0, -region_shift)
    region_high = jnp.minimum(HEIGHT, devices * BLOCK - region_shift)
    ccds = coef_ref.shape[0] // (V * NBASIS * 3)
    wide_lane = lax.broadcasted_iota(jnp.int32, (1, NBASIS * ROWS_IN), 1)

    def by_basis(value):
        total = jnp.full((1, NBASIS * ROWS_IN), value(0), jnp.float32)
        for basis in range(1, NBASIS):
            total = jnp.where(wide_lane >= basis * ROWS_IN, value(basis), total)
        return total

    def inside(first, count):
        rows = first + lax.broadcasted_iota(jnp.int32, (count, 1), 0)
        return (rows >= region_low) & (rows < region_high)

    depth = lax.broadcasted_iota(jnp.int32, (2 * BLOCK, BLOCK), 0)
    lane = lax.broadcasted_iota(jnp.int32, (2 * BLOCK, BLOCK), 1)
    distance = depth - (LEFT - HALF) - lane
    for basis in range(NBASIS):
        cols = pl.ds(basis * BLOCK, BLOCK)
        total = jnp.zeros((2 * BLOCK, BLOCK), jnp.float32)
        for tap in range(TAPS):
            total = jnp.where(
                distance == tap, taps_ref[(NBASIS + basis) * TAPS + tap], total
            )
        high, low = split(total)
        col_high[:, cols] = high
        col_low[:, cols] = low
    start = jnp.zeros((1, NBASIS * ROWS_IN), jnp.int32)
    for basis in range(1, NBASIS):
        start = jnp.where(wide_lane >= basis * ROWS_IN, basis * ROWS_IN, start)
    gap = (wide_lane - start) - lax.broadcasted_iota(
        jnp.int32, (ROWS_MID, NBASIS * ROWS_IN), 0
    )
    total = jnp.zeros(gap.shape, jnp.float32)
    for tap in range(TAPS):
        total = jnp.where(
            gap == tap, by_basis(lambda basis: taps_ref[basis * TAPS + tap]), total
        )
    row_kernel[...] = total
    wide[...] = jnp.zeros_like(wide)

    column = lax.broadcasted_iota(jnp.int32, (1, WIDTH), 1).astype(jnp.float32)
    col_pos = (2.0 * column + 1.0) / WIDTH - 1.0

    def remote(source, target, kind, step):
        return pltpu.make_async_remote_copy(
            src_ref=source,
            dst_ref=target,
            send_sem=sent.at[kind, step],
            recv_sem=received.at[kind, step],
            device_id={"ccd": lax.rem(band + step, devices)},
            device_id_type=pl.DeviceIdType.MESH,
        )

    pl.semaphore_wait(barrier, devices - 1)
    copies = [
        remote(meta_ref, metas_ref.at[band], CHUNKS, step) for step in outward(devices)
    ]
    locals_ = [pltpu.make_async_copy(meta_ref, metas_ref.at[band], own.at[CHUNKS])]
    for copy in copies + locals_:
        copy.start()
    for chunk in range(CHUNKS):
        first = top_row + chunk * CHUNK

        def one_visit(visit, carry, chunk=chunk, first=first):
            place = visit * ccds + ccd
            raw = jnp.concatenate([above_ref[visit], image_ref[visit], below_ref[visit]], axis=0)
            raw = raw[chunk * CHUNK : chunk * CHUNK + ROWS_IN]
            raw = jnp.where(inside(first - RIM, ROWS_IN), raw, 0.0)
            wide[:, LEFT : LEFT + WIDTH] = raw
            for block in range(BLKC):
                high, low = split(wide[:, block * BLOCK : (block + 2) * BLOCK])
                term = dot(high, col_high[...]) + dot(low, col_high[...]) + dot(high, col_low[...])
                high, low = split(term)
                for basis in range(NBASIS):
                    rows = pl.ds(basis * ROWS_IN, ROWS_IN)
                    cols = pl.ds(block * BLOCK, BLOCK)
                    terms_high[rows, cols] = high[:, basis * BLOCK : (basis + 1) * BLOCK]
                    terms_low[rows, cols] = low[:, basis * BLOCK : (basis + 1) * BLOCK]

            position = (first - REACH + lax.broadcasted_iota(jnp.int32, (ROWS_MID, 1), 0)).astype(
                jnp.float32
            )
            row_pos = (2.0 * position + 1.0) / HEIGHT - 1.0
            kernel = row_kernel[...]
            constant, by_row, by_column = (
                by_basis(lambda basis: coef_ref[(place * NBASIS + basis) * 3 + part]) for part in range(3)
            )
            level = kernel * (constant + by_row * row_pos)
            slope = kernel * by_column
            level_high, level_low = split(level)
            slope_high, slope_low = split(slope)
            upper = dot(
                jnp.concatenate([level_high, slope_high, level_low, slope_low], axis=0), terms_high[...]
            )
            lower = dot(jnp.concatenate([level_high, slope_high], axis=0), terms_low[...])
            both = upper[: 2 * ROWS_MID] + upper[2 * ROWS_MID :] + lower
            matched = both[:ROWS_MID] + both[ROWS_MID:] * col_pos
            mid[...] = jnp.where(inside(first - REACH, ROWS_MID), matched, 0.0)

            own_rows = (first + lax.broadcasted_iota(jnp.int32, (CHUNK, 1), 0)).astype(jnp.float32)
            row_shift = affine_ref[place * 4] + affine_ref[place * 4 + 1] * (
                (own_rows - (HEIGHT - 1) / 2.0) / HEIGHT
            )
            row_step = lax.broadcasted_iota(jnp.int32, (CHUNK, BLOCK), 1) - REACH
            row_weight = lanczos(row_shift - row_step.astype(jnp.float32))
            col_shift = affine_ref[place * 4 + 2] + affine_ref[place * 4 + 3] * (
                (column - (WIDTH - 1) / 2.0) / WIDTH
            )
            col_step = lax.broadcasted_iota(jnp.int32, (8, WIDTH), 0) - REACH
            reached = lax.broadcasted_iota(jnp.int32, (8, WIDTH), 1) + col_step
            col_weight = jnp.where(
                (reached >= 0) & (reached < WIDTH),
                lanczos(col_shift - col_step.astype(jnp.float32)),
                0.0,
            )
            warped = jnp.zeros((CHUNK, WIDTH), jnp.float32)
            for step in range(STEPS):
                warped = warped + row_weight[:, step : step + 1] * mid[step : step + CHUNK, :]
            total = jnp.zeros((CHUNK, WIDTH), jnp.float32)
            for step in range(STEPS):
                offset = step - REACH
                moved = warped if offset == 0 else pltpu.roll(warped, (-offset) % WIDTH, 1)
                total = total + col_weight[step : step + 1, :] * moved
            rounded = total.astype(jnp.bfloat16)
            for block in range(BLKC):
                stage[chunk * V * BLKC + visit * BLKC + block] = rounded[
                    :, block * BLOCK : (block + 1) * BLOCK
                ]
            return carry

        lax.fori_loop(0, V, one_visit, 0)
        for device in range(devices):
            for slot in range(capacity):
                outbox[chunk, device, slot] = stage[
                    chunk * V * BLKC + block_ref[device * capacity + slot]
                ]
        batch = [
            remote(
                outbox.at[chunk, lax.rem(band + step, devices)],
                got_ref.at[chunk, band],
                chunk,
                step,
            )
            for step in outward(devices)
        ]
        local = pltpu.make_async_copy(
            outbox.at[chunk, band], got_ref.at[chunk, band], own.at[chunk]
        )
        for copy in batch + [local]:
            copy.start()
        copies += batch
        locals_.append(local)
    for copy in locals_ + copies:
        copy.wait()


def gather_kernel(devices, capacity, meta_ref, owner_ref, weight_ref, got_ref, out_ref, total, weights):
    me = lax.axis_index("ccd")
    total[...] = jnp.zeros_like(total)
    for cell in range(PSIDE * PSIDE):
        weights[cell] = 0.0
    patch = jnp.int32(0)
    for candidate in range(owner_ref.shape[0]):
        patch = jnp.where(owner_ref[candidate] == me, candidate, patch)
    ccds = weight_ref.shape[0] // V
    count = V * BLKC

    def add(source, carry):
        ccd = (source + SPLIT // 2) // SPLIT
        taken = source * capacity
        for block in range(count):
            mine = meta_ref[source, 0, block] == patch

            @pl.when(mine)
            def _(taken=taken, block=block):
                cell = meta_ref[source, 0, count + block]
                weight = weight_ref[block // BLKC * ccds + ccd]
                weights[cell] = weights[cell] + weight
                for chunk in range(CHUNKS):
                    rows = pl.ds(chunk * CHUNK, CHUNK)
                    total[cell, rows] = total[cell, rows] + weight * got_ref[
                        chunk, taken
                    ].astype(jnp.float32)

            taken = taken + mine.astype(jnp.int32)
        return carry

    lax.fori_loop(0, devices, add, 0)
    for cell in range(PSIDE * PSIDE):
        row, col = cell // PSIDE * BLOCK, cell % PSIDE * BLOCK
        scale = jnp.full((1, BLOCK), jnp.maximum(weights[cell], 1.0), jnp.float32)
        out_ref[0, row : row + BLOCK, col : col + BLOCK] = total[cell] / scale


def shards(
    images, basis_taps, psf_coef, affine, visit_weight, block_patch, block_slot, patch_owner
):
    devices = lax.axis_size("ccd")
    block_count = V * BLKC
    capacity = max(2, (2 * block_count + devices - 1) // devices)
    slots = devices * capacity
    anywhere = pl.BlockSpec(memory_space=pl.ANY)
    scalars = pl.BlockSpec(memory_space=pltpu.SMEM)
    vector = pl.BlockSpec(memory_space=pltpu.VMEM)
    lanes = -(-2 * block_count // BLOCK) * BLOCK
    meta = jnp.pad(
        jnp.concatenate([block_patch[0, :, 0], block_slot[0]]), (0, lanes - 2 * block_count)
    )[None]
    rim_shape = jax.ShapeDtypeStruct((V, RIM, WIDTH), jnp.float32)
    above, below = pl.pallas_call(
        functools.partial(rim_kernel, devices),
        out_shape=(rim_shape, rim_shape),
        in_specs=[anywhere],
        out_specs=(anywhere, anywhere),
        scratch_shapes=[pltpu.SemaphoreType.DMA((4,))],
        compiler_params=pltpu.CompilerParams(collective_id=1, has_side_effects=True),
    )(images)

    blocks = pl.pallas_call(
        functools.partial(plan_kernel, devices, capacity),
        out_shape=jax.ShapeDtypeStruct((slots,), jnp.int32),
        in_specs=[scalars, scalars],
        out_specs=scalars,
        scratch_shapes=[pltpu.SMEM((devices,), jnp.int32)],
    )(block_patch.reshape(-1), patch_owner)
    metas, got = pl.pallas_call(
        functools.partial(band_kernel, devices, capacity),
        out_shape=(
            jax.ShapeDtypeStruct((devices, 1, lanes), jnp.int32),
            jax.ShapeDtypeStruct((CHUNKS, devices, capacity, CHUNK, BLOCK), jnp.bfloat16),
        ),
        in_specs=[scalars] * 4 + [vector] * 4,
        out_specs=(vector, anywhere),
        scratch_shapes=[
            pltpu.VMEM((2 * BLOCK, NBASIS * BLOCK), jnp.bfloat16),
            pltpu.VMEM((2 * BLOCK, NBASIS * BLOCK), jnp.bfloat16),
            pltpu.VMEM((ROWS_MID, NBASIS * ROWS_IN), jnp.float32),
            pltpu.VMEM((ROWS_IN, WIDTH + BLOCK), jnp.float32),
            pltpu.VMEM((NBASIS * ROWS_IN, WIDTH), jnp.bfloat16),
            pltpu.VMEM((NBASIS * ROWS_IN, WIDTH), jnp.bfloat16),
            pltpu.VMEM((ROWS_MID, WIDTH), jnp.float32),
            pltpu.VMEM((CHUNKS * block_count, CHUNK, BLOCK), jnp.bfloat16),
            pltpu.VMEM((CHUNKS, devices, capacity, CHUNK, BLOCK), jnp.bfloat16),
            pltpu.SemaphoreType.DMA((CHUNKS + 1, devices)),
            pltpu.SemaphoreType.DMA((CHUNKS + 1, devices)),
            pltpu.SemaphoreType.DMA((CHUNKS + 1,)),
        ],
        compiler_params=pltpu.CompilerParams(collective_id=2, has_side_effects=True),
    )(
        blocks,
        basis_taps.reshape(-1),
        psf_coef.reshape(-1),
        affine.reshape(-1),
        meta,
        above,
        images,
        below,
    )
    size = PSIDE * BLOCK
    return pl.pallas_call(
        functools.partial(gather_kernel, devices, capacity),
        out_shape=jax.ShapeDtypeStruct((1, size, size), jnp.float32),
        in_specs=[scalars, scalars, scalars, vector],
        out_specs=vector,
        scratch_shapes=[
            pltpu.VMEM((PSIDE * PSIDE, BLOCK, BLOCK), jnp.float32),
            pltpu.SMEM((PSIDE * PSIDE,), jnp.float32),
        ],
    )(metas, patch_owner, visit_weight.astype(jnp.float32).reshape(-1), got.reshape(CHUNKS, slots, CHUNK, BLOCK))


def solution(mesh):
    placed = (
        P(None, ("group", "ccd"), None),
        P(),
        P(None, "group", None, None),
        P(None, "group", None, None),
        P(None, "group"),
        P(("group", "ccd"), None, None),
        P(("group", "ccd"), None),
        P("group"),
    )
    return jax.shard_map(
        shards,
        mesh=mesh,
        in_specs=placed,
        out_specs=P(("group", "ccd"), None, None),
        check_vma=False,
    )
```

```python
import functools

import jax
import jax.numpy as jnp
from jax import lax
from jax.experimental import pallas as pl
from jax.experimental.pallas import tpu as pltpu
from jax.sharding import PartitionSpec as P

V = 4
BLOCK = 128
BLKC = 4
SPLIT = 4
TAPS = 11
NBASIS = 9
PSIDE = 4
HALF = TAPS // 2
REACH = 3
RIM = HALF + REACH
CHUNKS = 2
CHUNK = BLOCK // CHUNKS
ROWS_IN = CHUNK + 2 * RIM
ROWS_MID = CHUNK + 8
WIDTH = BLKC * BLOCK
HEIGHT = SPLIT * BLOCK
LEFT = BLOCK // 2
STEPS = 2 * REACH + 1


def sinc(values):
    angle = jnp.pi * values
    zero = values == 0.0
    return jnp.where(zero, 1.0, jnp.sin(angle) / jnp.where(zero, 1.0, angle))


def lanczos(offset):
    inside = jnp.abs(offset) < 3.0
    return jnp.where(inside, sinc(offset) * sinc(offset / 3.0), 0.0)


def outward(count):
    return sorted(range(1, count), key=lambda step: abs(step - count // 2))


def rim_kernel(count, image_ref, above_ref, below_ref, rims):
    me = lax.axis_index("ccd")
    barrier = pltpu.get_barrier_semaphore()
    has_next, has_last = me < count - 1, me > 0

    def to_next():
        return pltpu.make_async_remote_copy(
            src_ref=image_ref.at[:, pl.ds(BLOCK - RIM, RIM)],
            dst_ref=above_ref,
            send_sem=rims.at[0],
            recv_sem=rims.at[1],
            device_id={"ccd": lax.rem(me + 1, count)},
            device_id_type=pl.DeviceIdType.MESH,
        )

    def to_last():
        return pltpu.make_async_remote_copy(
            src_ref=image_ref.at[:, pl.ds(0, RIM)],
            dst_ref=below_ref,
            send_sem=rims.at[2],
            recv_sem=rims.at[3],
            device_id={"ccd": lax.rem(me + count - 1, count)},
            device_id_type=pl.DeviceIdType.MESH,
        )

    for present, step in ((has_next, 1), (has_last, count - 1)):

        @pl.when(present)
        def _(step=step):
            pl.semaphore_signal(
                barrier,
                inc=1,
                device_id={"ccd": lax.rem(me + step, count)},
                device_id_type=pl.DeviceIdType.MESH,
            )

    pl.semaphore_wait(barrier, has_next.astype(jnp.int32) + has_last.astype(jnp.int32))

    @pl.when(has_next)
    def _():
        to_next().start()

    @pl.when(has_last)
    def _():
        to_last().start()

    @pl.when(has_next)
    def _():
        to_next().wait_send()
        to_last().wait_recv()

    @pl.when(has_last)
    def _():
        to_last().wait_send()
        to_next().wait_recv()


def split(values):
    high = values.astype(jnp.bfloat16)
    return high, (values - high.astype(jnp.float32)).astype(jnp.bfloat16)


def dot(left, right):
    return jnp.dot(left, right, preferred_element_type=jnp.float32)


def plan_kernel(devices, capacity, patch_ref, slot_ref, owner_ref, block_ref, meta_ref, filled):
    for device in range(devices):
        filled[device] = 0
    for slot in range(devices * capacity):
        block_ref[slot] = 0
    lane = lax.broadcasted_iota(jnp.int32, meta_ref.shape, 1)
    meta = jnp.zeros(meta_ref.shape, jnp.int32)
    for block in range(V * BLKC):
        patch = patch_ref[block]
        meta = jnp.where(lane == block, patch, meta)
        meta = jnp.where(lane == V * BLKC + block, slot_ref[0, block], meta)
        device = owner_ref[patch]
        block_ref[device * capacity + filled[device]] = block
        filled[device] = filled[device] + 1
    meta_ref[...] = meta


def band_kernel(
    devices,
    capacity,
    block_ref,
    taps_ref,
    coef_ref,
    affine_ref,
    meta_ref,
    above_ref,
    image_ref,
    below_ref,
    metas_ref,
    got_ref,
    col_high,
    col_low,
    row_kernel,
    wide,
    terms_high,
    terms_low,
    mid,
    stage,
    outbox,
    sent,
    received,
    own,
):
    band = lax.axis_index("ccd")
    barrier = pltpu.get_barrier_semaphore()
    for step in range(1, devices):
        pl.semaphore_signal(
            barrier,
            inc=1,
            device_id={"ccd": lax.rem(band + step, devices)},
            device_id_type=pl.DeviceIdType.MESH,
        )
    shifted = band + SPLIT // 2
    ccd = shifted // SPLIT
    top_row = shifted % SPLIT * BLOCK
    region_shift = band * BLOCK - top_row
    region_low = jnp.maximum(0, -region_shift)
    region_high = jnp.minimum(HEIGHT, devices * BLOCK - region_shift)
    ccds = coef_ref.shape[0] // (V * NBASIS * 3)
    wide_lane = lax.broadcasted_iota(jnp.int32, (1, NBASIS * ROWS_IN), 1)

    def by_basis(value):
        total = jnp.full((1, NBASIS * ROWS_IN), value(0), jnp.float32)
        for basis in range(1, NBASIS):
            total = jnp.where(wide_lane >= basis * ROWS_IN, value(basis), total)
        return total

    def inside(first, count):
        rows = first + lax.broadcasted_iota(jnp.int32, (count, 1), 0)
        return (rows >= region_low) & (rows < region_high)

    depth = lax.broadcasted_iota(jnp.int32, (2 * BLOCK, BLOCK), 0)
    lane = lax.broadcasted_iota(jnp.int32, (2 * BLOCK, BLOCK), 1)
    distance = depth - (LEFT - HALF) - lane
    for basis in range(NBASIS):
        cols = pl.ds(basis * BLOCK, BLOCK)
        total = jnp.zeros((2 * BLOCK, BLOCK), jnp.float32)
        for tap in range(TAPS):
            total = jnp.where(
                distance == tap, taps_ref[1, basis, tap], total
            )
        high, low = split(total)
        col_high[:, cols] = high
        col_low[:, cols] = low
    start = jnp.zeros((1, NBASIS * ROWS_IN), jnp.int32)
    for basis in range(1, NBASIS):
        start = jnp.where(wide_lane >= basis * ROWS_IN, basis * ROWS_IN, start)
    gap = (wide_lane - start) - lax.broadcasted_iota(
        jnp.int32, (ROWS_MID, NBASIS * ROWS_IN), 0
    )
    total = jnp.zeros(gap.shape, jnp.float32)
    for tap in range(TAPS):
        total = jnp.where(
            gap == tap, by_basis(lambda basis: taps_ref[0, basis, tap]), total
        )
    row_kernel[...] = total
    wide[...] = jnp.zeros_like(wide)

    column = lax.broadcasted_iota(jnp.int32, (1, WIDTH), 1).astype(jnp.float32)
    col_pos = (2.0 * column + 1.0) / WIDTH - 1.0

    def remote(source, target, kind, step):
        return pltpu.make_async_remote_copy(
            src_ref=source,
            dst_ref=target,
            send_sem=sent.at[kind, step],
            recv_sem=received.at[kind, step],
            device_id={"ccd": lax.rem(band + step, devices)},
            device_id_type=pl.DeviceIdType.MESH,
        )

    pl.semaphore_wait(barrier, devices - 1)
    copies = [
        remote(meta_ref, metas_ref.at[band], CHUNKS, step) for step in outward(devices)
    ]
    locals_ = [pltpu.make_async_copy(meta_ref, metas_ref.at[band], own.at[CHUNKS])]
    for copy in copies + locals_:
        copy.start()
    for chunk in range(CHUNKS):
        first = top_row + chunk * CHUNK

        def one_visit(visit, carry, chunk=chunk, first=first):
            place = visit * ccds + ccd
            raw = jnp.concatenate([above_ref[visit], image_ref[visit], below_ref[visit]], axis=0)
            raw = raw[chunk * CHUNK : chunk * CHUNK + ROWS_IN]
            raw = jnp.where(inside(first - RIM, ROWS_IN), raw, 0.0)
            wide[:, LEFT : LEFT + WIDTH] = raw
            for block in range(BLKC):
                high, low = split(wide[:, block * BLOCK : (block + 2) * BLOCK])
                term = dot(high, col_high[...]) + dot(low, col_high[...]) + dot(high, col_low[...])
                high, low = split(term)
                for basis in range(NBASIS):
                    rows = pl.ds(basis * ROWS_IN, ROWS_IN)
                    cols = pl.ds(block * BLOCK, BLOCK)
                    terms_high[rows, cols] = high[:, basis * BLOCK : (basis + 1) * BLOCK]
                    terms_low[rows, cols] = low[:, basis * BLOCK : (basis + 1) * BLOCK]

            position = (first - REACH + lax.broadcasted_iota(jnp.int32, (ROWS_MID, 1), 0)).astype(
                jnp.float32
            )
            row_pos = (2.0 * position + 1.0) / HEIGHT - 1.0
            kernel = row_kernel[...]
            constant, by_row, by_column = (
                by_basis(lambda basis: coef_ref[(place * NBASIS + basis) * 3 + part]) for part in range(3)
            )
            level = kernel * (constant + by_row * row_pos)
            slope = kernel * by_column
            level_high, level_low = split(level)
            slope_high, slope_low = split(slope)
            upper = dot(
                jnp.concatenate([level_high, slope_high, level_low, slope_low], axis=0), terms_high[...]
            )
            lower = dot(jnp.concatenate([level_high, slope_high], axis=0), terms_low[...])
            both = upper[: 2 * ROWS_MID] + upper[2 * ROWS_MID :] + lower
            matched = both[:ROWS_MID] + both[ROWS_MID:] * col_pos
            mid[...] = jnp.where(inside(first - REACH, ROWS_MID), matched, 0.0)

            own_rows = (first + lax.broadcasted_iota(jnp.int32, (CHUNK, 1), 0)).astype(jnp.float32)
            row_shift = affine_ref[visit, ccd, 0, 0] + affine_ref[visit, ccd, 0, 1] * (
                (own_rows - (HEIGHT - 1) / 2.0) / HEIGHT
            )
            row_step = lax.broadcasted_iota(jnp.int32, (CHUNK, BLOCK), 1) - REACH
            row_weight = lanczos(row_shift - row_step.astype(jnp.float32))
            col_shift = affine_ref[visit, ccd, 1, 0] + affine_ref[visit, ccd, 1, 1] * (
                (column - (WIDTH - 1) / 2.0) / WIDTH
            )
            col_step = lax.broadcasted_iota(jnp.int32, (8, WIDTH), 0) - REACH
            reached = lax.broadcasted_iota(jnp.int32, (8, WIDTH), 1) + col_step
            col_weight = jnp.where(
                (reached >= 0) & (reached < WIDTH),
                lanczos(col_shift - col_step.astype(jnp.float32)),
                0.0,
            )
            warped = jnp.zeros((CHUNK, WIDTH), jnp.float32)
            for step in range(STEPS):
                warped = warped + row_weight[:, step : step + 1] * mid[step : step + CHUNK, :]
            total = jnp.zeros((CHUNK, WIDTH), jnp.float32)
            for step in range(STEPS):
                offset = step - REACH
                moved = warped if offset == 0 else pltpu.roll(warped, (-offset) % WIDTH, 1)
                total = total + col_weight[step : step + 1, :] * moved
            rounded = total.astype(jnp.bfloat16)
            for block in range(BLKC):
                stage[chunk * V * BLKC + visit * BLKC + block] = rounded[
                    :, block * BLOCK : (block + 1) * BLOCK
                ]
            return carry

        lax.fori_loop(0, V, one_visit, 0)
        for device in range(devices):
            for slot in range(capacity):
                outbox[chunk, device, slot] = stage[
                    chunk * V * BLKC + block_ref[device * capacity + slot]
                ]
        batch = [
            remote(
                outbox.at[chunk, lax.rem(band + step, devices)],
                got_ref.at[chunk, band],
                chunk,
                step,
            )
            for step in outward(devices)
        ]
        local = pltpu.make_async_copy(
            outbox.at[chunk, band], got_ref.at[chunk, band], own.at[chunk]
        )
        for copy in batch + [local]:
            copy.start()
        copies += batch
        locals_.append(local)
    for copy in locals_ + copies:
        copy.wait()


def gather_kernel(devices, capacity, meta_ref, owner_ref, weight_ref, got_ref, out_ref, total, weights):
    me = lax.axis_index("ccd")
    total[...] = jnp.zeros_like(total)
    for cell in range(PSIDE * PSIDE):
        weights[cell] = 0.0
    patch = jnp.int32(0)
    for candidate in range(owner_ref.shape[0]):
        patch = jnp.where(owner_ref[candidate] == me, candidate, patch)
    count = V * BLKC

    def add(source, carry):
        ccd = (source + SPLIT // 2) // SPLIT
        taken = source * capacity
        for block in range(count):
            mine = meta_ref[source, 0, block] == patch

            @pl.when(mine)
            def _(taken=taken, block=block):
                cell = meta_ref[source, 0, count + block]
                weight = weight_ref[block // BLKC, ccd]
                weights[cell] = weights[cell] + weight
                for chunk in range(CHUNKS):
                    rows = pl.ds(chunk * CHUNK, CHUNK)
                    total[cell, rows] = total[cell, rows] + weight * got_ref[
                        chunk, taken
                    ].astype(jnp.float32)

            taken = taken + mine.astype(jnp.int32)
        return carry

    lax.fori_loop(0, devices, add, 0)
    for cell in range(PSIDE * PSIDE):
        row, col = cell // PSIDE * BLOCK, cell % PSIDE * BLOCK
        scale = jnp.full((1, BLOCK), jnp.maximum(weights[cell], 1.0), jnp.float32)
        out_ref[0, row : row + BLOCK, col : col + BLOCK] = total[cell] / scale


def shards(
    images, basis_taps, psf_coef, affine, visit_weight, block_patch, block_slot, patch_owner
):
    devices = lax.axis_size("ccd")
    block_count = V * BLKC
    capacity = max(2, (2 * block_count + devices - 1) // devices)
    slots = devices * capacity
    anywhere = pl.BlockSpec(memory_space=pl.ANY)
    scalars = pl.BlockSpec(memory_space=pltpu.SMEM)
    vector = pl.BlockSpec(memory_space=pltpu.VMEM)
    lanes = -(-2 * block_count // BLOCK) * BLOCK
    rim_shape = jax.ShapeDtypeStruct((V, RIM, WIDTH), jnp.float32)
    above, below = pl.pallas_call(
        functools.partial(rim_kernel, devices),
        out_shape=(rim_shape, rim_shape),
        in_specs=[anywhere],
        out_specs=(anywhere, anywhere),
        scratch_shapes=[pltpu.SemaphoreType.DMA((4,))],
        compiler_params=pltpu.CompilerParams(collective_id=1, has_side_effects=True),
    )(images)

    blocks, meta = pl.pallas_call(
        functools.partial(plan_kernel, devices, capacity),
        out_shape=(
            jax.ShapeDtypeStruct((slots,), jnp.int32),
            jax.ShapeDtypeStruct((1, lanes), jnp.int32),
        ),
        in_specs=[scalars] * 3,
        out_specs=(scalars, vector),
        scratch_shapes=[pltpu.SMEM((devices,), jnp.int32)],
    )(block_patch.reshape(-1), block_slot, patch_owner)
    metas, got = pl.pallas_call(
        functools.partial(band_kernel, devices, capacity),
        out_shape=(
            jax.ShapeDtypeStruct((devices, 1, lanes), jnp.int32),
            jax.ShapeDtypeStruct((CHUNKS, devices, capacity, CHUNK, BLOCK), jnp.bfloat16),
        ),
        in_specs=[scalars] * 4 + [vector] * 4,
        out_specs=(vector, anywhere),
        scratch_shapes=[
            pltpu.VMEM((2 * BLOCK, NBASIS * BLOCK), jnp.bfloat16),
            pltpu.VMEM((2 * BLOCK, NBASIS * BLOCK), jnp.bfloat16),
            pltpu.VMEM((ROWS_MID, NBASIS * ROWS_IN), jnp.float32),
            pltpu.VMEM((ROWS_IN, WIDTH + BLOCK), jnp.float32),
            pltpu.VMEM((NBASIS * ROWS_IN, WIDTH), jnp.bfloat16),
            pltpu.VMEM((NBASIS * ROWS_IN, WIDTH), jnp.bfloat16),
            pltpu.VMEM((ROWS_MID, WIDTH), jnp.float32),
            pltpu.VMEM((CHUNKS * block_count, CHUNK, BLOCK), jnp.bfloat16),
            pltpu.VMEM((CHUNKS, devices, capacity, CHUNK, BLOCK), jnp.bfloat16),
            pltpu.SemaphoreType.DMA((CHUNKS + 1, devices)),
            pltpu.SemaphoreType.DMA((CHUNKS + 1, devices)),
            pltpu.SemaphoreType.DMA((CHUNKS + 1,)),
        ],
        compiler_params=pltpu.CompilerParams(collective_id=2, has_side_effects=True),
    )(
        blocks,
        basis_taps,
        psf_coef.reshape(-1),
        affine,
        meta,
        above,
        images,
        below,
    )
    size = PSIDE * BLOCK
    return pl.pallas_call(
        functools.partial(gather_kernel, devices, capacity),
        out_shape=jax.ShapeDtypeStruct((1, size, size), jnp.float32),
        in_specs=[scalars, scalars, scalars, vector],
        out_specs=vector,
        scratch_shapes=[
            pltpu.VMEM((PSIDE * PSIDE, BLOCK, BLOCK), jnp.float32),
            pltpu.SMEM((PSIDE * PSIDE,), jnp.float32),
        ],
    )(metas, patch_owner, visit_weight.astype(jnp.float32), got.reshape(CHUNKS, slots, CHUNK, BLOCK))


def solution(mesh):
    placed = (
        P(None, ("group", "ccd"), None),
        P(),
        P(None, "group", None, None),
        P(None, "group", None, None),
        P(None, "group"),
        P(("group", "ccd"), None, None),
        P(("group", "ccd"), None),
        P("group"),
    )
    return jax.shard_map(
        shards,
        mesh=mesh,
        in_specs=placed,
        out_specs=P(("group", "ccd"), None, None),
        check_vma=False,
    )
```

```python
import functools

import jax
import jax.numpy as jnp
from jax import lax
from jax.experimental import pallas as pl
from jax.experimental.pallas import tpu as pltpu
from jax.sharding import PartitionSpec as P

V = 4
BLOCK = 128
BLKC = 4
SPLIT = 4
TAPS = 11
NBASIS = 9
PSIDE = 4
HALF = TAPS // 2
REACH = 3
RIM = HALF + REACH
CHUNKS = 2
CHUNK = BLOCK // CHUNKS
ROWS_IN = CHUNK + 2 * RIM
ROWS_MID = CHUNK + 8
WIDTH = BLKC * BLOCK
HEIGHT = SPLIT * BLOCK
LEFT = BLOCK // 2
STEPS = 2 * REACH + 1


def sinc(values):
    angle = jnp.pi * values
    zero = values == 0.0
    return jnp.where(zero, 1.0, jnp.sin(angle) / jnp.where(zero, 1.0, angle))


def lanczos(offset):
    inside = jnp.abs(offset) < 3.0
    return jnp.where(inside, sinc(offset) * sinc(offset / 3.0), 0.0)


def outward(count):
    far = sorted(range(1, count), key=lambda step: abs(step - count // 2))
    half = len(far) // 2
    near = far[half:][::-1]
    mixed = [step for pair in zip(far[:half], near) for step in pair]
    return mixed + near[half:]


def rim_kernel(count, image_ref, above_ref, below_ref, rims):
    me = lax.axis_index("ccd")
    barrier = pltpu.get_barrier_semaphore()
    has_next, has_last = me < count - 1, me > 0

    def to_next():
        return pltpu.make_async_remote_copy(
            src_ref=image_ref.at[:, pl.ds(BLOCK - RIM, RIM)],
            dst_ref=above_ref,
            send_sem=rims.at[0],
            recv_sem=rims.at[1],
            device_id={"ccd": lax.rem(me + 1, count)},
            device_id_type=pl.DeviceIdType.MESH,
        )

    def to_last():
        return pltpu.make_async_remote_copy(
            src_ref=image_ref.at[:, pl.ds(0, RIM)],
            dst_ref=below_ref,
            send_sem=rims.at[2],
            recv_sem=rims.at[3],
            device_id={"ccd": lax.rem(me + count - 1, count)},
            device_id_type=pl.DeviceIdType.MESH,
        )

    for present, step in ((has_next, 1), (has_last, count - 1)):

        @pl.when(present)
        def _(step=step):
            pl.semaphore_signal(
                barrier,
                inc=1,
                device_id={"ccd": lax.rem(me + step, count)},
                device_id_type=pl.DeviceIdType.MESH,
            )

    pl.semaphore_wait(barrier, has_next.astype(jnp.int32) + has_last.astype(jnp.int32))

    @pl.when(has_next)
    def _():
        to_next().start()

    @pl.when(has_last)
    def _():
        to_last().start()

    @pl.when(has_next)
    def _():
        to_next().wait_send()
        to_last().wait_recv()

    @pl.when(has_last)
    def _():
        to_last().wait_send()
        to_next().wait_recv()


def split(values):
    high = values.astype(jnp.bfloat16)
    return high, (values - high.astype(jnp.float32)).astype(jnp.bfloat16)


def dot(left, right):
    return jnp.dot(left, right, preferred_element_type=jnp.float32)


def plan_kernel(devices, capacity, patch_ref, slot_ref, owner_ref, block_ref, meta_ref, filled):
    for device in range(devices):
        filled[device] = 0
    for slot in range(devices * capacity):
        block_ref[slot] = 0
    lane = lax.broadcasted_iota(jnp.int32, meta_ref.shape, 1)
    meta = jnp.zeros(meta_ref.shape, jnp.int32)
    for block in range(V * BLKC):
        patch = patch_ref[block]
        meta = jnp.where(lane == block, patch, meta)
        meta = jnp.where(lane == V * BLKC + block, slot_ref[0, block], meta)
        device = owner_ref[patch]
        block_ref[device * capacity + filled[device]] = block
        filled[device] = filled[device] + 1
    meta_ref[...] = meta


def band_kernel(
    devices,
    capacity,
    block_ref,
    taps_ref,
    coef_ref,
    affine_ref,
    meta_ref,
    above_ref,
    image_ref,
    below_ref,
    metas_ref,
    got_ref,
    col_high,
    col_low,
    row_kernel,
    wide,
    terms_high,
    terms_low,
    mid,
    stage,
    outbox,
    sent,
    received,
    own,
):
    band = lax.axis_index("ccd")
    barrier = pltpu.get_barrier_semaphore()
    for step in range(1, devices):
        pl.semaphore_signal(
            barrier,
            inc=1,
            device_id={"ccd": lax.rem(band + step, devices)},
            device_id_type=pl.DeviceIdType.MESH,
        )
    shifted = band + SPLIT // 2
    ccd = shifted // SPLIT
    top_row = shifted % SPLIT * BLOCK
    region_shift = band * BLOCK - top_row
    region_low = jnp.maximum(0, -region_shift)
    region_high = jnp.minimum(HEIGHT, devices * BLOCK - region_shift)
    ccds = coef_ref.shape[0] // (V * NBASIS * 3)
    wide_lane = lax.broadcasted_iota(jnp.int32, (1, NBASIS * ROWS_IN), 1)

    def by_basis(value):
        total = jnp.full((1, NBASIS * ROWS_IN), value(0), jnp.float32)
        for basis in range(1, NBASIS):
            total = jnp.where(wide_lane >= basis * ROWS_IN, value(basis), total)
        return total

    def inside(first, count):
        rows = first + lax.broadcasted_iota(jnp.int32, (count, 1), 0)
        return (rows >= region_low) & (rows < region_high)

    depth = lax.broadcasted_iota(jnp.int32, (2 * BLOCK, BLOCK), 0)
    lane = lax.broadcasted_iota(jnp.int32, (2 * BLOCK, BLOCK), 1)
    distance = depth - (LEFT - HALF) - lane
    for basis in range(NBASIS):
        cols = pl.ds(basis * BLOCK, BLOCK)
        total = jnp.zeros((2 * BLOCK, BLOCK), jnp.float32)
        for tap in range(TAPS):
            total = jnp.where(
                distance == tap, taps_ref[1, basis, tap], total
            )
        high, low = split(total)
        col_high[:, cols] = high
        col_low[:, cols] = low
    start = jnp.zeros((1, NBASIS * ROWS_IN), jnp.int32)
    for basis in range(1, NBASIS):
        start = jnp.where(wide_lane >= basis * ROWS_IN, basis * ROWS_IN, start)
    gap = (wide_lane - start) - lax.broadcasted_iota(
        jnp.int32, (ROWS_MID, NBASIS * ROWS_IN), 0
    )
    total = jnp.zeros(gap.shape, jnp.float32)
    for tap in range(TAPS):
        total = jnp.where(
            gap == tap, by_basis(lambda basis: taps_ref[0, basis, tap]), total
        )
    row_kernel[...] = total
    wide[...] = jnp.zeros_like(wide)

    column = lax.broadcasted_iota(jnp.int32, (1, WIDTH), 1).astype(jnp.float32)
    col_pos = (2.0 * column + 1.0) / WIDTH - 1.0

    def remote(source, target, kind, step):
        return pltpu.make_async_remote_copy(
            src_ref=source,
            dst_ref=target,
            send_sem=sent.at[kind, step],
            recv_sem=received.at[kind, step],
            device_id={"ccd": lax.rem(band + step, devices)},
            device_id_type=pl.DeviceIdType.MESH,
        )

    pl.semaphore_wait(barrier, devices - 1)
    copies = [
        remote(meta_ref, metas_ref.at[band], CHUNKS, step) for step in outward(devices)
    ]
    locals_ = [pltpu.make_async_copy(meta_ref, metas_ref.at[band], own.at[CHUNKS])]
    for copy in copies + locals_:
        copy.start()
    for chunk in range(CHUNKS):
        first = top_row + chunk * CHUNK

        def one_visit(visit, carry, chunk=chunk, first=first):
            place = visit * ccds + ccd
            raw = jnp.concatenate([above_ref[visit], image_ref[visit], below_ref[visit]], axis=0)
            raw = raw[chunk * CHUNK : chunk * CHUNK + ROWS_IN]
            raw = jnp.where(inside(first - RIM, ROWS_IN), raw, 0.0)
            wide[:, LEFT : LEFT + WIDTH] = raw
            for block in range(BLKC):
                high, low = split(wide[:, block * BLOCK : (block + 2) * BLOCK])
                term = dot(high, col_high[...]) + dot(low, col_high[...]) + dot(high, col_low[...])
                high, low = split(term)
                for basis in range(NBASIS):
                    rows = pl.ds(basis * ROWS_IN, ROWS_IN)
                    cols = pl.ds(block * BLOCK, BLOCK)
                    terms_high[rows, cols] = high[:, basis * BLOCK : (basis + 1) * BLOCK]
                    terms_low[rows, cols] = low[:, basis * BLOCK : (basis + 1) * BLOCK]

            position = (first - REACH + lax.broadcasted_iota(jnp.int32, (ROWS_MID, 1), 0)).astype(
                jnp.float32
            )
            row_pos = (2.0 * position + 1.0) / HEIGHT - 1.0
            kernel = row_kernel[...]
            constant, by_row, by_column = (
                by_basis(lambda basis: coef_ref[(place * NBASIS + basis) * 3 + part]) for part in range(3)
            )
            level = kernel * (constant + by_row * row_pos)
            slope = kernel * by_column
            level_high, level_low = split(level)
            slope_high, slope_low = split(slope)
            upper = dot(
                jnp.concatenate([level_high, slope_high, level_low, slope_low], axis=0), terms_high[...]
            )
            lower = dot(jnp.concatenate([level_high, slope_high], axis=0), terms_low[...])
            both = upper[: 2 * ROWS_MID] + upper[2 * ROWS_MID :] + lower
            matched = both[:ROWS_MID] + both[ROWS_MID:] * col_pos
            mid[...] = jnp.where(inside(first - REACH, ROWS_MID), matched, 0.0)

            own_rows = (first + lax.broadcasted_iota(jnp.int32, (CHUNK, 1), 0)).astype(jnp.float32)
            row_shift = affine_ref[visit, ccd, 0, 0] + affine_ref[visit, ccd, 0, 1] * (
                (own_rows - (HEIGHT - 1) / 2.0) / HEIGHT
            )
            row_step = lax.broadcasted_iota(jnp.int32, (CHUNK, BLOCK), 1) - REACH
            row_weight = lanczos(row_shift - row_step.astype(jnp.float32))
            col_shift = affine_ref[visit, ccd, 1, 0] + affine_ref[visit, ccd, 1, 1] * (
                (column - (WIDTH - 1) / 2.0) / WIDTH
            )
            col_step = lax.broadcasted_iota(jnp.int32, (8, WIDTH), 0) - REACH
            reached = lax.broadcasted_iota(jnp.int32, (8, WIDTH), 1) + col_step
            col_weight = jnp.where(
                (reached >= 0) & (reached < WIDTH),
                lanczos(col_shift - col_step.astype(jnp.float32)),
                0.0,
            )
            warped = jnp.zeros((CHUNK, WIDTH), jnp.float32)
            for step in range(STEPS):
                warped = warped + row_weight[:, step : step + 1] * mid[step : step + CHUNK, :]
            total = jnp.zeros((CHUNK, WIDTH), jnp.float32)
            for step in range(STEPS):
                offset = step - REACH
                moved = warped if offset == 0 else pltpu.roll(warped, (-offset) % WIDTH, 1)
                total = total + col_weight[step : step + 1, :] * moved
            rounded = total.astype(jnp.bfloat16)
            for block in range(BLKC):
                stage[chunk * V * BLKC + visit * BLKC + block] = rounded[
                    :, block * BLOCK : (block + 1) * BLOCK
                ]
            return carry

        lax.fori_loop(0, V, one_visit, 0)
        for device in range(devices):
            for slot in range(capacity):
                outbox[chunk, device, slot] = stage[
                    chunk * V * BLKC + block_ref[device * capacity + slot]
                ]
        batch = [
            remote(
                outbox.at[chunk, lax.rem(band + step, devices)],
                got_ref.at[chunk, band],
                chunk,
                step,
            )
            for step in outward(devices)
        ]
        local = pltpu.make_async_copy(
            outbox.at[chunk, band], got_ref.at[chunk, band], own.at[chunk]
        )
        for copy in batch + [local]:
            copy.start()
        copies += batch
        locals_.append(local)
    for copy in locals_ + copies:
        copy.wait()


def gather_kernel(devices, capacity, meta_ref, owner_ref, weight_ref, got_ref, out_ref, total, weights):
    me = lax.axis_index("ccd")
    total[...] = jnp.zeros_like(total)
    for cell in range(PSIDE * PSIDE):
        weights[cell] = 0.0
    patch = jnp.int32(0)
    for candidate in range(owner_ref.shape[0]):
        patch = jnp.where(owner_ref[candidate] == me, candidate, patch)
    count = V * BLKC

    def add(source, carry):
        ccd = (source + SPLIT // 2) // SPLIT
        taken = source * capacity
        for block in range(count):
            mine = meta_ref[source, 0, block] == patch

            @pl.when(mine)
            def _(taken=taken, block=block):
                cell = meta_ref[source, 0, count + block]
                weight = weight_ref[block // BLKC, ccd]
                weights[cell] = weights[cell] + weight
                for chunk in range(CHUNKS):
                    rows = pl.ds(chunk * CHUNK, CHUNK)
                    total[cell, rows] = total[cell, rows] + weight * got_ref[
                        chunk, taken
                    ].astype(jnp.float32)

            taken = taken + mine.astype(jnp.int32)
        return carry

    lax.fori_loop(0, devices, add, 0)
    for cell in range(PSIDE * PSIDE):
        row, col = cell // PSIDE * BLOCK, cell % PSIDE * BLOCK
        scale = jnp.full((1, BLOCK), jnp.maximum(weights[cell], 1.0), jnp.float32)
        out_ref[0, row : row + BLOCK, col : col + BLOCK] = total[cell] / scale


def shards(
    images, basis_taps, psf_coef, affine, visit_weight, block_patch, block_slot, patch_owner
):
    devices = lax.axis_size("ccd")
    block_count = V * BLKC
    capacity = max(2, (2 * block_count + devices - 1) // devices)
    slots = devices * capacity
    anywhere = pl.BlockSpec(memory_space=pl.ANY)
    scalars = pl.BlockSpec(memory_space=pltpu.SMEM)
    vector = pl.BlockSpec(memory_space=pltpu.VMEM)
    lanes = -(-2 * block_count // BLOCK) * BLOCK
    rim_shape = jax.ShapeDtypeStruct((V, RIM, WIDTH), jnp.float32)
    above, below = pl.pallas_call(
        functools.partial(rim_kernel, devices),
        out_shape=(rim_shape, rim_shape),
        in_specs=[anywhere],
        out_specs=(anywhere, anywhere),
        scratch_shapes=[pltpu.SemaphoreType.DMA((4,))],
        compiler_params=pltpu.CompilerParams(collective_id=1, has_side_effects=True),
    )(images)

    blocks, meta = pl.pallas_call(
        functools.partial(plan_kernel, devices, capacity),
        out_shape=(
            jax.ShapeDtypeStruct((slots,), jnp.int32),
            jax.ShapeDtypeStruct((1, lanes), jnp.int32),
        ),
        in_specs=[scalars] * 3,
        out_specs=(scalars, vector),
        scratch_shapes=[pltpu.SMEM((devices,), jnp.int32)],
    )(block_patch.reshape(-1), block_slot, patch_owner)
    metas, got = pl.pallas_call(
        functools.partial(band_kernel, devices, capacity),
        out_shape=(
            jax.ShapeDtypeStruct((devices, 1, lanes), jnp.int32),
            jax.ShapeDtypeStruct((CHUNKS, devices, capacity, CHUNK, BLOCK), jnp.bfloat16),
        ),
        in_specs=[scalars] * 4 + [vector] * 4,
        out_specs=(vector, anywhere),
        scratch_shapes=[
            pltpu.VMEM((2 * BLOCK, NBASIS * BLOCK), jnp.bfloat16),
            pltpu.VMEM((2 * BLOCK, NBASIS * BLOCK), jnp.bfloat16),
            pltpu.VMEM((ROWS_MID, NBASIS * ROWS_IN), jnp.float32),
            pltpu.VMEM((ROWS_IN, WIDTH + BLOCK), jnp.float32),
            pltpu.VMEM((NBASIS * ROWS_IN, WIDTH), jnp.bfloat16),
            pltpu.VMEM((NBASIS * ROWS_IN, WIDTH), jnp.bfloat16),
            pltpu.VMEM((ROWS_MID, WIDTH), jnp.float32),
            pltpu.VMEM((CHUNKS * block_count, CHUNK, BLOCK), jnp.bfloat16),
            pltpu.VMEM((CHUNKS, devices, capacity, CHUNK, BLOCK), jnp.bfloat16),
            pltpu.SemaphoreType.DMA((CHUNKS + 1, devices)),
            pltpu.SemaphoreType.DMA((CHUNKS + 1, devices)),
            pltpu.SemaphoreType.DMA((CHUNKS + 1,)),
        ],
        compiler_params=pltpu.CompilerParams(collective_id=2, has_side_effects=True),
    )(
        blocks,
        basis_taps,
        psf_coef.reshape(-1),
        affine,
        meta,
        above,
        images,
        below,
    )
    size = PSIDE * BLOCK
    return pl.pallas_call(
        functools.partial(gather_kernel, devices, capacity),
        out_shape=jax.ShapeDtypeStruct((1, size, size), jnp.float32),
        in_specs=[scalars, scalars, scalars, vector],
        out_specs=vector,
        scratch_shapes=[
            pltpu.VMEM((PSIDE * PSIDE, BLOCK, BLOCK), jnp.float32),
            pltpu.SMEM((PSIDE * PSIDE,), jnp.float32),
        ],
    )(metas, patch_owner, visit_weight.astype(jnp.float32), got.reshape(CHUNKS, slots, CHUNK, BLOCK))


def solution(mesh):
    placed = (
        P(None, ("group", "ccd"), None),
        P(),
        P(None, "group", None, None),
        P(None, "group", None, None),
        P(None, "group"),
        P(("group", "ccd"), None, None),
        P(("group", "ccd"), None),
        P("group"),
    )
    return jax.shard_map(
        shards,
        mesh=mesh,
        in_specs=placed,
        out_specs=P(("group", "ccd"), None, None),
        check_vma=False,
    )
```
